512 devices in a mesh: wide: 64 (over z, y), narrow: 8 (over x, core).
Axes of the slice: x: 4, y: 4, z: 16, core: 2. Of those that a mesh axis runs over, the one named last changes fastest.
Arguments:
- embeddings: bfloat16 [768, 8192], P('wide', 'narrow'), may hold values from -6 to 6
- norm_gain: bfloat16 [8192], P('narrow'), may hold values from 0.25 to 1.75
- query_weight: bfloat16 [8192, 8192], P('narrow', 'wide'), may hold values from -1 to 1, as said below
- key_weight: bfloat16 [8192, 1024], P('narrow', 'wide'), may hold values from -1 to 1, as said below
- value_weight: bfloat16 [8192, 1024], P('narrow', 'wide'), may hold values from -0.0625 to 0.0625
- output_weight: bfloat16 [8192, 8192], P('wide', 'narrow'), may hold values from -0.0625 to 0.0625
- segment_ids: int32 [768], replicated, may hold values from 0 to 5, never falling along the last dimension, each value on 1 to 250 neighbouring positions
- cotangent: bfloat16 [768, 8192], P('wide', 'narrow'), may hold values from -6 to 6
Outputs:
- grad_input: bfloat16 [768, 8192], P('wide', 'narrow')
The draws below stay inside these ranges and needn't reach their ends.
Inputs may be any that keep to these rules, and one draw needn't show every extreme that they name: `segment_ids`: segment ids never fall along the tokens; each candidate's tokens are contiguous, and one candidate has exactly min(250, 763) tokens. `query_weight`: entries of order 8192 ** -0.5. `key_weight`: entries of order 8192 ** -0.5.
All inputs are finite; a program needn't handle non-finite values.
Results may differ from the reference program's by a relative error of at most 0.0095.
The reference program's roundings to bfloat16 on the way count: a program that leaves them out, or rounds other values in their place, can miss the bound.
Values may be sent and summed in bfloat16 or wider, within the bound.
A program may use at most 64 MiB of HBM per device.

```python
import math
import jax
import jax.numpy as jnp
import numpy as np
from jax import lax

D = 8192
HEADS = 64
KV_HEADS = 8
HDIM = 128
TOKENS = 768
MOST = 250
CANDS = 6
QW = 8192
KVD = 1024


def shared_weights(key):
    query_key = jax.random.fold_in(key, 101)
    other_key = jax.random.fold_in(key, 202)
    query = jnp.clip(jax.random.normal(query_key, (D, HEADS * HDIM), jnp.float32), -6.0, 6.0) / D ** 0.5
    keys = jnp.clip(jax.random.normal(other_key, (D, KV_HEADS * HDIM), jnp.float32), -6.0, 6.0) / D ** 0.5
    return (query, keys)


def draw_query_weight(key, part):
    return shared_weights(key)[0].astype(jnp.bfloat16)


def draw_key_weight(key, part):
    return shared_weights(key)[1].astype(jnp.bfloat16)


def shard_levels(rng, dims, shards, least, high):
    def one(axis_at, blocks):
        heights = jax.random.uniform(jax.random.fold_in(jax.random.fold_in(rng, 6), axis_at), (blocks,), jnp.float32, least / len(shards), high / len(shards))
        return jnp.repeat(jnp.exp(heights), dims[axis_at] // blocks).reshape((-1,) + (1,) * (len(dims) - axis_at - 1))

    level = one(*shards[0])
    for cut in shards[1:]:
        level = level * one(*cut)
    return level


def profile(number_of, total, most, slope):
    portions = [(1 << 20) // math.isqrt(standing ** slope) + 1 for standing in range(2, number_of + 1)]
    rest, holding = total - most - (number_of - 1), [1] * (number_of - 1)
    while rest > 0:
        movable = [i for i in range(number_of - 1) if holding[i] < most]
        mass, budget = sum([portions[i] for i in movable]), rest
        for i in movable:
            extra = min(most - holding[i], max(1, budget * portions[i] // mass), rest)
            holding[i] = holding[i] + extra
            rest = rest - extra
    return np.array([most] + holding)


def ragged(rng, count, total, bound, skew):
    if count == 2:
        one = jax.random.randint(rng, (), max(1, total - bound), min(bound, total - 1) + 1)
        return jnp.stack([one, total - one])
    tallies = jnp.asarray(profile(count, total, bound, skew), jnp.int32)
    couples = (count - 1) // 2
    donor, receiver = tallies[1:1 + 2 * couples:2], tallies[2:2 + 2 * couples:2]
    room = jnp.minimum(donor - 1, bound - receiver)
    moved = jax.random.randint(jax.random.fold_in(rng, 1), (couples,), 0, 1 << 20) % (room + 1)
    tallies = tallies.at[1:1 + 2 * couples:2].set(donor - moved).at[2:2 + 2 * couples:2].set(receiver + moved)
    return tallies[jax.random.permutation(jax.random.fold_in(rng, 2), count)]


def scatter_about(key, extent, scale, reach, split=(), held_as=jnp.bfloat16):
    level = shard_levels(key, extent, split, -0.22, 0.18) if split else 1.0
    drawn = jax.random.normal(key, extent, jnp.float32) * scale * level
    return jnp.minimum(jnp.maximum(drawn, -reach), reach).astype(held_as)


def setup_inputs(seed: int = 0) -> dict:
    key_list = jax.random.split(jax.random.key(seed), 9)
    embeddings = scatter_about(key_list[0], (TOKENS, D), 1.0, 6.0, ((0, 64), (1, 8)))
    norm_gain = jnp.clip(1.0 + 0.15 * jax.random.normal(key_list[1], (D,), jnp.float32), 0.25, 1.75).astype(jnp.bfloat16)
    query_weight = draw_query_weight(jax.random.fold_in(key_list[8], 71), 0)
    key_weight = draw_key_weight(jax.random.fold_in(key_list[8], 71), 0)
    value_weight = scatter_about(key_list[4], (D, KVD), D ** -0.5, 0.0625, ((0, 8), (1, 64)))
    output_weight = scatter_about(key_list[5], (QW, D), QW ** -0.5, 0.0625, ((0, 64), (1, 8)))
    segment_ids = jnp.searchsorted(jnp.cumsum(ragged(key_list[6], CANDS, TOKENS, min(MOST, TOKENS - CANDS + 1), 1)), jnp.arange(TOKENS), side="right").astype(jnp.int32)
    cotangent = scatter_about(key_list[7], (TOKENS, D), 1.0, 6.0, ((0, 64), (1, 8)))
    return dict(embeddings=embeddings, norm_gain=norm_gain, query_weight=query_weight, key_weight=key_weight, value_weight=value_weight, output_weight=output_weight, segment_ids=segment_ids, cotangent=cotangent)


EPS = 1e-05
THETA = 500000.0

def rotary_tables(segment_ids, head_size):
    count = segment_ids.shape[0]
    places = jnp.arange(count, dtype=jnp.int32)
    earlier = jnp.concatenate([jnp.full((1,), -1, jnp.int32), segment_ids[:-1]])
    starts = lax.cummax(jnp.where(segment_ids != earlier, places, 0), axis=0)
    position = (places - starts).astype(jnp.float32)
    half = head_size // 2
    frequency = jnp.exp(-(2.0 * jnp.arange(half, dtype=jnp.float32) / head_size) * math.log(THETA))
    angle = position[:, None] * frequency[None, :]
    return (jnp.cos(angle), jnp.sin(angle))

def rotate(values, cosine, sine):
    half = values.shape[1] // 2
    first, second = (values[:, :half], values[:, half:])
    return jnp.concatenate([first * cosine - second * sine, second * cosine + first * sine], 1)

def unrotate(values, cosine, sine):
    half = values.shape[1] // 2
    first, second = (values[:, :half], values[:, half:])
    return jnp.concatenate([first * cosine + second * sine, second * cosine - first * sine], 1)

def head_grads(query_rows, keys, values, grad_rows, allowed, scale):
    scores = lax.dot_general(query_rows, keys, (((1,), (1,)), ((), ())), preferred_element_type=jnp.float32) * scale
    scores = jnp.where(allowed, scores, -1e+30)
    highest = lax.optimization_barrier(jnp.max(scores, 1, keepdims=True))
    raised = jnp.exp(scores - highest)
    attend = raised / lax.optimization_barrier(jnp.sum(raised, 1, keepdims=True))
    attend_low = attend.astype(jnp.bfloat16)
    grad_attend = lax.dot_general(grad_rows, values, (((1,), (1,)), ((), ())), preferred_element_type=jnp.float32)
    centre = lax.optimization_barrier(jnp.sum(attend * grad_attend, 1, keepdims=True))
    grad_scores = (attend * (grad_attend - centre) * scale).astype(jnp.bfloat16)
    grad_query = jnp.dot(grad_scores, keys, preferred_element_type=jnp.float32)
    grad_key = lax.dot_general(grad_scores, query_rows, (((0,), (0,)), ((), ())), preferred_element_type=jnp.float32)
    grad_value = lax.dot_general(attend_low, grad_rows, (((0,), (0,)), ((), ())), preferred_element_type=jnp.float32)
    return (grad_query, grad_key, grad_value)

def reference(embeddings, norm_gain, query_weight, key_weight, value_weight, output_weight, segment_ids, cotangent):
    group = HEADS // KV_HEADS
    scale = HDIM ** (-0.5)
    inputs = embeddings.astype(jnp.float32)
    gain = norm_gain.astype(jnp.float32)
    inverse = lax.rsqrt(lax.optimization_barrier(jnp.sum(inputs * inputs, 1, keepdims=True)) / D + EPS)
    normed = (inputs * inverse * gain).astype(jnp.bfloat16)
    queries_pre = jnp.dot(normed, query_weight, preferred_element_type=jnp.float32)
    keys_pre = jnp.dot(normed, key_weight, preferred_element_type=jnp.float32)
    values = jnp.dot(normed, value_weight, preferred_element_type=jnp.float32).astype(jnp.bfloat16)
    grad_heads = jnp.dot(cotangent, output_weight.T, preferred_element_type=jnp.float32).astype(jnp.bfloat16)
    cosine, sine = rotary_tables(segment_ids, HDIM)
    places = jnp.arange(TOKENS, dtype=jnp.int32)
    allowed = (segment_ids[:, None] == segment_ids[None, :]) & (places[None, :] <= places[:, None])
    keys_all = jnp.stack([rotate(keys_pre[:, g * HDIM:(g + 1) * HDIM], cosine, sine) for g in range(KV_HEADS)]).astype(jnp.bfloat16)
    values_all = values.reshape(TOKENS, KV_HEADS, HDIM).transpose(1, 0, 2)
    queries_all = queries_pre.reshape(TOKENS, HEADS, HDIM).transpose(1, 0, 2)
    grads_all = grad_heads.reshape(TOKENS, HEADS, HDIM).transpose(1, 0, 2)

    def one_head(head):
        key_head = head // group
        query_rows = rotate(queries_all[head], cosine, sine).astype(jnp.bfloat16)
        grad_query, grad_key, grad_value = head_grads(query_rows, keys_all[key_head], values_all[key_head], grads_all[head], allowed, scale)
        return (unrotate(grad_query, cosine, sine).astype(jnp.bfloat16), unrotate(grad_key, cosine, sine).astype(jnp.bfloat16), grad_value.astype(jnp.bfloat16))
    grad_query, grad_key, grad_value = lax.map(one_head, jnp.arange(HEADS, dtype=jnp.int32))
    query_matrix = grad_query.transpose(1, 0, 2).reshape(TOKENS, HEADS * HDIM)
    key_sum = grad_key.astype(jnp.float32).reshape(KV_HEADS, group, TOKENS, HDIM).sum(1).transpose(1, 0, 2).reshape(TOKENS, KV_HEADS * HDIM)
    value_sum = grad_value.astype(jnp.float32).reshape(KV_HEADS, group, TOKENS, HDIM).sum(1).transpose(1, 0, 2).reshape(TOKENS, KV_HEADS * HDIM)
    grad_normed = jnp.dot(query_matrix, query_weight.T, preferred_element_type=jnp.float32)
    grad_normed = grad_normed + jnp.dot(key_sum, key_weight.astype(jnp.float32).T, precision=lax.Precision.HIGHEST)
    grad_normed = grad_normed + jnp.dot(value_sum, value_weight.astype(jnp.float32).T, precision=lax.Precision.HIGHEST)
    scaled = grad_normed * gain
    inner = lax.optimization_barrier(jnp.sum(scaled * inputs, 1, keepdims=True))
    result = inverse * scaled - inputs * inverse * inverse * inverse * (inner / D)
    return result.astype(jnp.bfloat16)
```

```python
import functools
import math

import jax
import jax.numpy as jnp
from jax import lax
from jax.experimental import pallas as pl
from jax.experimental.pallas import tpu as pltpu
from jax.sharding import PartitionSpec as P

D = 8192
HDIM = 128
EPS = 1e-05
THETA = 500000.0
MESH = pl.DeviceIdType.MESH
Y = 4
X = 4
F32 = jnp.float32
BF16 = jnp.bfloat16


def remote(src, dst, send, recv, **where):
    return pltpu.make_async_remote_copy(
        src_ref=src, dst_ref=dst, send_sem=send, recv_sem=recv, device_id=where, device_id_type=MESH
    )


def meet(peers):
    barrier = pltpu.get_barrier_semaphore()
    for where in peers:
        pl.semaphore_signal(barrier, inc=1, device_id=where, device_id_type=MESH)
    pl.semaphore_wait(barrier, len(peers))


def places(zs):
    w, n = lax.axis_index("wide"), lax.axis_index("narrow")
    z, y = w // Y, w % Y
    ypeer = [z * Y + (y + k) % Y for k in range(Y)]
    up, down = ((z + 1) % zs) * Y + y, ((z + zs - 1) % zs) * Y + y
    npeer = [(n + k) % (2 * X) for k in range(2 * X)]
    return z, y, n, ypeer, up, down, npeer


def exchange_sums(value, n, npeer, own, slots, send, recv):
    own[...] = value
    slots[n] = value
    copies = [
        remote(own, slots.at[n], send.at[k], recv.at[k], narrow=npeer[k]) for k in range(1, len(npeer))
    ]
    for copy in copies:
        copy.start()
    return copies


def gather_kernel(
    zs, emb, gain, cot, kw, vw,
    e_out, c_out, k_out, v_out, inv_out,
    sq_own, sq, ey, cy, stage,
    sq_s, sq_r, y_s, y_r, ring_s, ring_r, kv_s, kv_r,
):
    z, y, n, ypeer, up, down, npeer = places(zs)
    rows = emb.shape[0]
    half = zs // 2
    meet([dict(narrow=npeer[k]) for k in range(1, 2 * X)]
         + [dict(wide=ypeer[k]) for k in range(1, Y)] + [dict(wide=up), dict(wide=down)])

    started = []

    def go(copy):
        copy.start()
        started.append(copy)
        return copy

    cot_y = [go(remote(cot, cy.at[y], y_s.at[0, k], y_r.at[0, k], wide=ypeer[k])) for k in range(1, Y)]
    x = emb[...].astype(F32)
    part = jnp.broadcast_to(jnp.sum(x * x, 1, keepdims=True), (rows, 128))
    sums = exchange_sums(part, n, npeer, sq_own, sq, sq_s, sq_r)
    slot = (z % 2) * Y + y
    kv_y = []
    for k in range(1, Y):
        kv_y.append(go(remote(kw, k_out.at[slot], y_s.at[2, k], y_r.at[2, k], wide=ypeer[k])))
        kv_y.append(go(remote(vw, v_out.at[slot], y_s.at[3, k], y_r.at[3, k], wide=ypeer[k])))
    k_out[slot] = kw[...]
    v_out[slot] = vw[...]
    cy[y] = cot[...]

    def settle(copies, blocks, out):
        for copy in copies:
            copy.wait_recv()
        for j in range(Y):
            stage[rows * j : rows * (j + 1), :] = blocks[j].astype(F32)
        out[z] = stage[...].astype(BF16)

    ring = {}

    def step(a, s):
        ref = (c_out, e_out)[a]
        for way in range(2):
            if s > 0 and (way, a, s - 1) in ring:
                ring[way, a, s - 1].wait_recv()
            if s == half - 1 and a != way:
                continue
            block = (z + zs - s) % zs if way == 0 else (z + s) % zs
            ring[way, a, s] = go(
                remote(
                    ref.at[block], ref.at[block], ring_s.at[way, a, s], ring_r.at[way, a, s],
                    wide=(up, down)[way],
                )
            )

    settle(cot_y, cy, c_out)
    step(0, 0)
    for copy in sums:
        copy.wait()
    total = sq[0]
    for k in range(1, 2 * X):
        total = total + sq[k]
    inverse = lax.rsqrt(total / D + EPS)
    inv_out[...] = inverse
    ey[y] = (x * inverse[:, :1] * gain[...].astype(F32)).astype(BF16)
    emb_y = [go(remote(ey.at[y], ey.at[y], y_s.at[1, k], y_r.at[1, k], wide=ypeer[k])) for k in range(1, Y)]
    settle(emb_y, ey, e_out)
    step(1, 0)
    pair = []
    for s in range(1, half):
        step(0, s)
        step(1, s)
        if s == 1:
            for copy in kv_y:
                copy.wait_recv()
            twin = (z + 1 - 2 * (z % 2)) * Y + y
            mine = pl.ds((z % 2) * Y, Y)
            pair = [
                go(remote(ref.at[mine], ref.at[mine], kv_s.at[i], kv_r.at[i], wide=twin))
                for i, ref in enumerate((k_out, v_out))
            ]
    for a in range(2):
        ring[a, a, half - 1].wait_recv()
    for copy in pair:
        copy.wait_recv()
    for copy in started:
        copy.wait_send()


def gather(zs, emb, gain, cot, kw, vw):
    rows, width = emb.shape
    vmem = pl.BlockSpec(memory_space=pltpu.VMEM)
    block = Y * rows
    dma = pltpu.SemaphoreType.DMA
    return pl.pallas_call(
        functools.partial(gather_kernel, zs),
        out_shape=(
            jax.ShapeDtypeStruct((zs, block, width), BF16),
            jax.ShapeDtypeStruct((zs, block, width), BF16),
            jax.ShapeDtypeStruct((2 * Y,) + kw.shape, BF16),
            jax.ShapeDtypeStruct((2 * Y,) + vw.shape, BF16),
            jax.ShapeDtypeStruct((rows, 128), F32),
        ),
        in_specs=[vmem] * 5,
        out_specs=(vmem,) * 5,
        scratch_shapes=[
            pltpu.VMEM((rows, 128), F32),
            pltpu.VMEM((2 * X, rows, 128), F32),
            pltpu.VMEM((Y, rows, width), BF16),
            pltpu.VMEM((Y, rows, width), BF16),
            pltpu.VMEM((block, width), F32),
            dma((2 * X,)), dma((2 * X,)),
            dma((4, Y)), dma((4, Y)),
            dma((2, 2, zs // 2)), dma((2, 2, zs // 2)),
            dma((2,)), dma((2,)),
        ],
        compiler_params=pltpu.CompilerParams(collective_id=0, has_side_effects=True),
        name="gather",
    )(emb, gain, cot, kw, vw)


def reduce_kernel(
    part, cosine, sine, out,
    pbuf, sbuf, rbuf,
    p_s, p_r, x_s, x_r, gx_s, gx_r, gp_s, gp_r,
):
    n = lax.axis_index("narrow")
    x, core = n // 2, n % 2
    twin = x * 2 + 1 - core
    xs = [(x + k) % X for k in range(X)]
    meet([dict(narrow=twin)] + [dict(narrow=xs[k] * 2 + core) for k in range(1, X)])
    order = (2, 1, 3, 0)
    started = []

    def go(copy):
        copy.start()
        started.append(copy)
        return copy

    first = {
        k: go(remote(part.at[1 - core, xs[k]], pbuf.at[xs[k]], p_s.at[k], p_r.at[k], narrow=twin))
        for k in order
    }
    across = {}
    for k in order:
        first[k].wait_recv()
        sbuf[xs[k]] = part[core, xs[k]] + pbuf[xs[k]]
        if k:
            across[k] = go(
                remote(sbuf.at[xs[k]], rbuf.at[k], x_s.at[k], x_r.at[k], narrow=xs[k] * 2 + core)
            )
    total = sbuf[x]
    for k in (1, 3, 2):
        across[k].wait_recv()
        total = total + rbuf[k]
    cos, sin = cosine[core, x], sine[core, x]
    for i in range(4):
        value = total[:, i * HDIM : (i + 1) * HDIM]
        if i < 2:
            value = value * cos + pltpu.roll(value, HDIM // 2, 1) * sin
        out[core, x, :, i * HDIM : (i + 1) * HDIM] = value.astype(BF16)
    mine = out.at[core, x]
    given = {
        k: go(remote(mine, mine, gx_s.at[k], gx_r.at[k], narrow=xs[k] * 2 + core)) for k in (2, 1, 3)
    }
    shared = [go(remote(mine, mine, gp_s.at[0], gp_r.at[0], narrow=twin))]
    for k in (1, 3, 2):
        given[k].wait_recv()
        block = out.at[core, (x + X - k) % X]
        shared.append(go(remote(block, block, gp_s.at[k], gp_r.at[k], narrow=twin)))
    for copy in shared:
        copy.wait_recv()
    for copy in started:
        copy.wait_send()


def reduce_narrow(part, cosine, sine):
    tokens, cols = part.shape
    chunk = tokens // (2 * X)
    vmem = pl.BlockSpec(memory_space=pltpu.VMEM)
    dma = pltpu.SemaphoreType.DMA
    out = pl.pallas_call(
        reduce_kernel,
        out_shape=jax.ShapeDtypeStruct((2, X, chunk, cols), BF16),
        in_specs=[vmem] * 3,
        out_specs=vmem,
        scratch_shapes=[
            pltpu.VMEM((X, chunk, cols), F32),
            pltpu.VMEM((X, chunk, cols), F32),
            pltpu.VMEM((X, chunk, cols), F32),
        ]
        + [dma((X,))] * 8,
        compiler_params=pltpu.CompilerParams(collective_id=1, has_side_effects=True),
        name="reduce",
    )(
        part.reshape(2, X, chunk, cols),
        cosine.reshape(2, X, chunk, HDIM),
        sine.reshape(2, X, chunk, HDIM),
    )
    return out.reshape(tokens, cols)


def scatter_kernel(
    zs, gn, emb, gain, inv, out,
    sbuf, rbuf, stage, ysend, yrecv, in_own, inn,
    z_s, z_r, y_s, y_r, n_s, n_r,
):
    z, y, n, ypeer, up, down, npeer = places(zs)
    rows, width = emb.shape
    half, wid = zs // 2, width // 2
    meet([dict(narrow=npeer[k]) for k in range(1, 2 * X)]
         + [dict(wide=ypeer[k]) for k in range(1, Y)] + [dict(wide=up), dict(wide=down)])
    started = []

    def go(copy):
        copy.start()
        started.append(copy)
        return copy

    chain = {}
    lanes = [slice(h * wid, (h + 1) * wid) for h in range(2)]
    for s in range(half):
        for h in range(2):
            for way in range(2):
                length = half if h == way else half - 1
                if s >= length:
                    continue
                far = length - s
                block = (z + far) % zs if way == 0 else (z + zs - far) % zs
                value = gn[block, :, lanes[h]]
                if s:
                    chain[way, h].wait_recv()
                    value = value + rbuf[way, h, s - 1].astype(F32)
                sbuf[way, h, s] = value.astype(BF16)
                chain[way, h] = go(
                    remote(
                        sbuf.at[way, h, s], rbuf.at[way, h, s], z_s.at[way, h, s], z_r.at[way, h, s],
                        wide=(up, down)[way],
                    )
                )
    for h in range(2):
        value = gn[z, :, lanes[h]]
        for way in range(2):
            length = half if h == way else half - 1
            chain[way, h].wait_recv()
            value = value + rbuf[way, h, length - 1].astype(F32)
        stage[:, lanes[h]] = value
    for j in range(Y):
        ysend[j] = stage[rows * j : rows * (j + 1), :]
    yrecv[y] = ysend[y]
    last = [
        go(remote(ysend.at[(y + k) % Y], yrecv.at[y], y_s.at[k], y_r.at[k], wide=ypeer[k]))
        for k in range(1, Y)
    ]
    for copy in last:
        copy.wait_recv()
    scaled = (yrecv[0] + yrecv[1] + yrecv[2] + yrecv[3]) * gain[...].astype(F32)
    inputs = emb[...].astype(F32)
    part = jnp.broadcast_to(jnp.sum(scaled * inputs, 1, keepdims=True), (rows, 128))
    sums = exchange_sums(part, n, npeer, in_own, inn, n_s, n_r)
    for copy in sums:
        copy.wait()
    inner = inn[0]
    for k in range(1, 2 * X):
        inner = inner + inn[k]
    inverse = inv[...]
    slope = (inverse * inverse * inverse * (inner / D))[:, :1]
    out[...] = (inverse[:, :1] * scaled - inputs * slope).astype(BF16)
    for copy in started:
        copy.wait_send()


def scatter(zs, gn, emb, gain, inv):
    rows, width = emb.shape
    block = Y * rows
    vmem = pl.BlockSpec(memory_space=pltpu.VMEM)
    dma = pltpu.SemaphoreType.DMA
    half = zs // 2
    return pl.pallas_call(
        functools.partial(scatter_kernel, zs),
        out_shape=jax.ShapeDtypeStruct((rows, width), BF16),
        in_specs=[vmem] * 4,
        out_specs=vmem,
        scratch_shapes=[
            pltpu.VMEM((2, 2, half, block, width // 2), BF16),
            pltpu.VMEM((2, 2, half, block, width // 2), BF16),
            pltpu.VMEM((block, width), F32),
            pltpu.VMEM((Y, rows, width), F32),
            pltpu.VMEM((Y, rows, width), F32),
            pltpu.VMEM((rows, 128), F32),
            pltpu.VMEM((2 * X, rows, 128), F32),
            dma((2, 2, half)), dma((2, 2, half)),
            dma((Y,)), dma((Y,)),
            dma((2 * X,)), dma((2 * X,)),
        ],
        compiler_params=pltpu.CompilerParams(collective_id=2, has_side_effects=True),
        name="scatter",
    )(gn.reshape(zs, block, width), emb, gain, inv)


def rotary_tables(segment_ids):
    spots = jnp.arange(segment_ids.shape[0], dtype=jnp.int32)
    starts = jnp.sum((segment_ids[None, :] < segment_ids[:, None]).astype(jnp.int32), 1)
    position = (spots - starts).astype(F32)
    half = HDIM // 2
    frequency = jnp.exp(-(2.0 * jnp.arange(half, dtype=F32) / HDIM) * math.log(THETA))
    angle = position[:, None] * frequency[None, :]
    cosine, sine = jnp.cos(angle), jnp.sin(angle)
    return jnp.concatenate([cosine, cosine], 1), jnp.concatenate([-sine, sine], 1)


def swap(values):
    half = HDIM // 2
    return jnp.concatenate([values[:, half:], values[:, :half]], 1)


def dot(a, b, da, db):
    return lax.dot_general(a, b, (((da,), (db,)), ((), ())), preferred_element_type=F32)


def head_grads(q, k, v, g, allowed, scale):
    scores = jnp.where(allowed, dot(q, k, 1, 1) * scale, -1e30)
    raised = jnp.exp(scores - jnp.max(scores, 1, keepdims=True))
    attend = raised / jnp.sum(raised, 1, keepdims=True)
    grad_attend = dot(g, v, 1, 1)
    centre = jnp.sum(attend * grad_attend, 1, keepdims=True)
    grad_scores = (attend * (grad_attend - centre) * scale).astype(BF16)
    return (
        dot(grad_scores, k, 1, 0),
        dot(grad_scores, q, 0, 0),
        dot(attend.astype(BF16), g, 0, 0),
    )


def local(emb, norm_gain, query_weight, key_weight, value_weight, output_weight, segment_ids, cot):
    zs = lax.axis_size("wide") // Y
    total = segment_ids.shape[0]
    gain = norm_gain[None, :]
    e_all, c_all, kt, vt, inv = gather(zs, emb, gain, cot, key_weight.T, value_weight.T)
    width = emb.shape[1]
    e_all, c_all = e_all.reshape(total, width), c_all.reshape(total, width)
    kt, vt = kt.reshape(HDIM, width), vt.reshape(HDIM, width)
    cosine, sine = rotary_tables(segment_ids)
    part = jnp.concatenate(
        [
            dot(e_all, query_weight, 1, 0),
            dot(e_all, kt, 1, 1),
            dot(e_all, vt, 1, 1),
            dot(c_all, output_weight, 1, 1),
        ],
        1,
    )
    heads = reduce_narrow(part, cosine, sine)
    q, k, v, g = (heads[:, i * HDIM : (i + 1) * HDIM] for i in range(4))
    spots = jnp.arange(total, dtype=jnp.int32)
    allowed = (segment_ids[:, None] == segment_ids[None, :]) & (spots[None, :] <= spots[:, None])
    gq, gk, gv = head_grads(q, k, v, g, allowed, HDIM ** (-0.5))
    gq = (gq * cosine - swap(gq) * sine).astype(BF16)
    gk = (gk * cosine - swap(gk) * sine).astype(BF16)
    gn = dot(gq, query_weight, 1, 1) + dot(gk, kt, 1, 0) + dot(gv.astype(BF16), vt, 1, 0)
    return scatter(zs, gn, emb, gain, inv)


def solution(mesh):
    return jax.shard_map(
        local,
        mesh=mesh,
        in_specs=(
            P("wide", "narrow"),
            P("narrow"),
            P("narrow", "wide"),
            P("narrow", "wide"),
            P("narrow", "wide"),
            P("wide", "narrow"),
            P(),
            P("wide", "narrow"),
        ),
        out_specs=P("wide", "narrow"),
        check_vma=False,
    )
```

```python
import functools
import math

import jax
import jax.numpy as jnp
from jax import lax
from jax.experimental import pallas as pl
from jax.experimental.pallas import tpu as pltpu
from jax.sharding import PartitionSpec as P

D = 8192
HDIM = 128
EPS = 1e-05
THETA = 500000.0
MESH = pl.DeviceIdType.MESH
Y = 4
X = 4
F32 = jnp.float32
BF16 = jnp.bfloat16


def remote(src, dst, send, recv, **where):
    return pltpu.make_async_remote_copy(
        src_ref=src, dst_ref=dst, send_sem=send, recv_sem=recv, device_id=where, device_id_type=MESH
    )


def meet(peers):
    barrier = pltpu.get_barrier_semaphore()
    for where in peers:
        pl.semaphore_signal(barrier, inc=1, device_id=where, device_id_type=MESH)
    pl.semaphore_wait(barrier, len(peers))


def places(zs):
    w, n = lax.axis_index("wide"), lax.axis_index("narrow")
    z, y = w // Y, w % Y
    ypeer = [z * Y + (y + k) % Y for k in range(Y)]
    up, down = ((z + 1) % zs) * Y + y, ((z + zs - 1) % zs) * Y + y
    npeer = [(n + k) % (2 * X) for k in range(2 * X)]
    return z, y, n, ypeer, up, down, npeer


def exchange_sums(value, n, npeer, own, slots, send, recv):
    own[...] = value
    slots[n] = value
    copies = [
        remote(own, slots.at[n], send.at[k], recv.at[k], narrow=npeer[k]) for k in range(1, len(npeer))
    ]
    for copy in copies:
        copy.start()
    return copies


def gather_kernel(
    zs, emb, gain, cot, kw, vw,
    e_out, c_out, k_out, v_out, inv_out,
    sq_own, sq, ey, cy, stage,
    sq_s, sq_r, y_s, y_r, wide_s, wide_r, thin_s, thin_r, spread_s, spread_r, kv_s, kv_r,
):
    z, y, n, ypeer, up, down, npeer = places(zs)
    rows, width = emb.shape
    half, wid = zs // 2, width // 2
    part = wid // Y
    outs = (c_out, e_out)
    twin = (z + 1 - 2 * (z % 2)) * Y + y
    meet([dict(narrow=npeer[k]) for k in range(1, 2 * X)]
         + [dict(wide=ypeer[k]) for k in range(1, Y)] + [dict(wide=up), dict(wide=down)])

    started = []

    def go(copy):
        copy.start()
        started.append(copy)
        return copy

    cot_y = [go(remote(cot, cy.at[y], y_s.at[0, k], y_r.at[0, k], wide=ypeer[k])) for k in range(1, Y)]
    x = emb[...].astype(F32)
    squares = jnp.broadcast_to(jnp.sum(x * x, 1, keepdims=True), (rows, 128))
    sums = exchange_sums(squares, n, npeer, sq_own, sq, sq_s, sq_r)
    slot = (z % 2) * Y + y
    pair = [
        go(remote(src, dst.at[slot], kv_s.at[i], kv_r.at[i], wide=twin))
        for i, (src, dst) in enumerate(((kw, k_out), (vw, v_out)))
    ]
    k_out[slot] = kw[...]
    v_out[slot] = vw[...]
    cy[y] = cot[...]

    def settle(copies, blocks, out):
        for copy in copies:
            copy.wait_recv()
        for j in range(Y):
            stage[rows * j : rows * (j + 1), :] = blocks[j].astype(F32)
        out[z] = stage[...].astype(BF16)

    def step(ring, view, sems, a, s):
        if s > 0:
            for way in range(2):
                if (way, a, s - 1) in ring:
                    ring[way, a, s - 1].wait_recv()
        for way in range(2):
            if s >= half or (s == half - 1 and a != way):
                continue
            here = view(outs[a], (z + zs - s) % zs if way == 0 else (z + s) % zs)
            ring[way, a, s] = go(
                remote(here, here, sems[0].at[way, a, s], sems[1].at[way, a, s], wide=(up, down)[way])
            )

    broad, thin = {}, {}

    def broad_step(a, s):
        step(broad, lambda ref, block: ref.at[block, :, 0:wid], (wide_s, wide_r), a, s)

    def lane(yy):
        return pl.ds(pl.multiple_of(wid + part * yy, 128), part)

    def thin_step(s):
        for a in range(2):
            step(thin, lambda ref, block: ref.at[block, :, lane(y)], (thin_s, thin_r), a, s)

    def y_send(i, j, here, k):
        return go(remote(here, here, spread_s.at[i, j], spread_r.at[i, j], wide=ypeer[k]))

    def spread(i, view):
        first = [y_send(i, j, view(j % 2, y), 1 if j < 2 else Y - 1) for j in range(4)]
        return [i, view, first]

    def relay(item):
        i, view, first = item
        first[0].wait_recv()
        first[3].wait_recv()
        item.append(y_send(i, 4, view(0, (y + Y - 1) % Y), 1))
        item.append(y_send(i, 5, view(1, (y + 1) % Y), Y - 1))

    def finish(item):
        item[2][1].wait_recv()
        item[2][2].wait_recv()
        item[3].wait_recv()
        item[4].wait_recv()

    def thin_view(block):
        return lambda a, yy: outs[a].at[block, :, lane(yy)]

    def kv_view(base):
        return lambda a, yy: (k_out, v_out)[a].at[base + yy]

    settle(cot_y, cy, c_out)
    broad_step(0, 0)
    for copy in sums:
        copy.wait()
    total = sq[0]
    for k in range(1, 2 * X):
        total = total + sq[k]
    inverse = lax.rsqrt(total / D + EPS)
    inv_out[...] = inverse
    ey[y] = (x * inverse[:, :1] * gain[...].astype(F32)).astype(BF16)
    emb_y = [go(remote(ey.at[y], ey.at[y], y_s.at[1, k], y_r.at[1, k], wide=ypeer[k])) for k in range(1, Y)]
    settle(emb_y, ey, e_out)
    count = 2 * half - 1
    items, relayed = [], 0

    def spread_after(s):
        if s < half - 1:
            items.append(spread(2 * s, thin_view((z + zs - s - 1) % zs)))
            items.append(spread(2 * s + 1, thin_view((z + s + 1) % zs)))
        else:
            items.append(spread(2 * s, thin_view((z + half) % zs)))

    for s in range(half):
        ready = len(items)
        if 2 * s <= half:
            thin_step(2 * s)
            if s > 0:
                spread_after(2 * s - 1)
        if s > 0:
            broad_step(0, s)
        broad_step(1, s)
        if 2 * s + 1 <= half:
            thin_step(2 * s + 1)
            spread_after(2 * s)
        for item in items[relayed:ready]:
            relay(item)
        relayed = max(relayed, ready)
        if s == 0:
            for copy in pair:
                copy.wait_recv()
            items.append(spread(count, kv_view((z % 2) * Y)))
            items.append(spread(count + 1, kv_view(Y - (z % 2) * Y)))
    for item in items[relayed:]:
        relay(item)
    for item in items:
        finish(item)
    for a in range(2):
        broad[a, a, half - 1].wait_recv()
    for copy in started:
        copy.wait_send()


def gather(zs, emb, gain, cot, kw, vw):
    rows, width = emb.shape
    vmem = pl.BlockSpec(memory_space=pltpu.VMEM)
    block = Y * rows
    dma = pltpu.SemaphoreType.DMA
    return pl.pallas_call(
        functools.partial(gather_kernel, zs),
        out_shape=(
            jax.ShapeDtypeStruct((zs, block, width), BF16),
            jax.ShapeDtypeStruct((zs, block, width), BF16),
            jax.ShapeDtypeStruct((2 * Y,) + kw.shape, BF16),
            jax.ShapeDtypeStruct((2 * Y,) + vw.shape, BF16),
            jax.ShapeDtypeStruct((rows, 128), F32),
        ),
        in_specs=[vmem] * 5,
        out_specs=(vmem,) * 5,
        scratch_shapes=[
            pltpu.VMEM((rows, 128), F32),
            pltpu.VMEM((2 * X, rows, 128), F32),
            pltpu.VMEM((Y, rows, width), BF16),
            pltpu.VMEM((Y, rows, width), BF16),
            pltpu.VMEM((block, width), F32),
            dma((2 * X,)), dma((2 * X,)),
            dma((2, Y)), dma((2, Y)),
            dma((2, 2, zs // 2)), dma((2, 2, zs // 2)),
            dma((2, 2, zs // 2)), dma((2, 2, zs // 2)),
            dma((zs + 1, 6)), dma((zs + 1, 6)),
            dma((2,)), dma((2,)),
        ],
        compiler_params=pltpu.CompilerParams(collective_id=0, has_side_effects=True),
        name="gather",
    )(emb, gain, cot, kw, vw)


def reduce_kernel(
    e_all, c_all, qw, kt, vt, ow, cosine, sine, out,
    away, home, pbuf, sbuf, rbuf,
    p_s, p_r, x_s, x_r, gx_s, gx_r, gp_s, gp_r,
):
    n = lax.axis_index("narrow")
    x, core = n // 2, n % 2
    twin = x * 2 + 1 - core
    xs = [(x + k) % X for k in range(X)]
    meet([dict(narrow=twin)] + [dict(narrow=xs[k] * 2 + core) for k in range(1, X)])
    order = (2, 1, 3, 0)
    started = []

    def go(copy):
        copy.start()
        started.append(copy)
        return copy

    def project(side, into):
        e, c = e_all[side], c_all[side]
        for i, (rows, weight, over) in enumerate(((e, qw, 0), (e, kt, 1), (e, vt, 1), (c, ow, 1))):
            value = dot(rows, weight[...], 1, over)
            into[:, :, i * HDIM : (i + 1) * HDIM] = value.reshape(into.shape[:2] + (HDIM,))

    project(1 - core, away)
    first = {
        k: go(remote(away.at[xs[k]], pbuf.at[xs[k]], p_s.at[k], p_r.at[k], narrow=twin))
        for k in order
    }
    project(core, home)
    across = {}
    for k in order:
        first[k].wait_recv()
        sbuf[xs[k]] = home[xs[k]] + pbuf[xs[k]]
        if k:
            across[k] = go(
                remote(sbuf.at[xs[k]], rbuf.at[k], x_s.at[k], x_r.at[k], narrow=xs[k] * 2 + core)
            )
    total = sbuf[x]
    for k in (1, 3, 2):
        across[k].wait_recv()
        total = total + rbuf[k]
    cos, sin = cosine[core, x], sine[core, x]
    for i in range(4):
        value = total[:, i * HDIM : (i + 1) * HDIM]
        if i < 2:
            value = value * cos + pltpu.roll(value, HDIM // 2, 1) * sin
        out[core, x, :, i * HDIM : (i + 1) * HDIM] = value.astype(BF16)
    mine = out.at[core, x]
    given = {
        k: go(remote(mine, mine, gx_s.at[k], gx_r.at[k], narrow=xs[k] * 2 + core)) for k in (2, 1, 3)
    }
    shared = [go(remote(mine, mine, gp_s.at[0], gp_r.at[0], narrow=twin))]
    for k in (1, 3, 2):
        given[k].wait_recv()
        block = out.at[core, (x + X - k) % X]
        shared.append(go(remote(block, block, gp_s.at[k], gp_r.at[k], narrow=twin)))
    for copy in shared:
        copy.wait_recv()
    for copy in started:
        copy.wait_send()


def reduce_narrow(e_all, c_all, qw, kt, vt, ow, cosine, sine):
    tokens, cols = cosine.shape[0], 4 * HDIM
    chunk = tokens // (2 * X)
    vmem = pl.BlockSpec(memory_space=pltpu.VMEM)
    dma = pltpu.SemaphoreType.DMA
    out = pl.pallas_call(
        reduce_kernel,
        out_shape=jax.ShapeDtypeStruct((2, X, chunk, cols), BF16),
        in_specs=[vmem] * 8,
        out_specs=vmem,
        scratch_shapes=[pltpu.VMEM((X, chunk, cols), F32)] * 5 + [dma((X,))] * 8,
        compiler_params=pltpu.CompilerParams(collective_id=1, has_side_effects=True),
        name="reduce",
    )(
        e_all.reshape(2, X * chunk, -1),
        c_all.reshape(2, X * chunk, -1),
        qw, kt, vt, ow,
        cosine.reshape(2, X, chunk, HDIM),
        sine.reshape(2, X, chunk, HDIM),
    )
    return out.reshape(tokens, cols)


def scatter_kernel(
    zs, gn, emb, gain, inv, out,
    sbuf, rbuf, stage, ysend, yrecv, in_own, inn,
    z_s, z_r, y_s, y_r, n_s, n_r,
):
    z, y, n, ypeer, up, down, npeer = places(zs)
    rows, width = emb.shape
    half, wid = zs // 2, width // 2
    meet([dict(narrow=npeer[k]) for k in range(1, 2 * X)]
         + [dict(wide=ypeer[k]) for k in range(1, Y)] + [dict(wide=up), dict(wide=down)])
    started = []

    def go(copy):
        copy.start()
        started.append(copy)
        return copy

    chain = {}
    lanes = [slice(h * wid, (h + 1) * wid) for h in range(2)]
    for s in range(half):
        for h in range(2):
            for way in range(2):
                length = half if h == way else half - 1
                if s >= length:
                    continue
                far = length - s
                block = (z + far) % zs if way == 0 else (z + zs - far) % zs
                value = gn[block, :, lanes[h]]
                if s:
                    chain[way, h].wait_recv()
                    value = value + rbuf[way, h, s - 1].astype(F32)
                sbuf[way, h, s] = value.astype(BF16)
                chain[way, h] = go(
                    remote(
                        sbuf.at[way, h, s], rbuf.at[way, h, s], z_s.at[way, h, s], z_r.at[way, h, s],
                        wide=(up, down)[way],
                    )
                )
    for h in range(2):
        value = gn[z, :, lanes[h]]
        for way in range(2):
            length = half if h == way else half - 1
            chain[way, h].wait_recv()
            value = value + rbuf[way, h, length - 1].astype(F32)
        stage[:, lanes[h]] = value
    for j in range(Y):
        ysend[j] = stage[rows * j : rows * (j + 1), :]
    yrecv[y] = ysend[y]
    last = [
        go(remote(ysend.at[(y + k) % Y], yrecv.at[y], y_s.at[k], y_r.at[k], wide=ypeer[k]))
        for k in range(1, Y)
    ]
    for copy in last:
        copy.wait_recv()
    scaled = (yrecv[0] + yrecv[1] + yrecv[2] + yrecv[3]) * gain[...].astype(F32)
    inputs = emb[...].astype(F32)
    part = jnp.broadcast_to(jnp.sum(scaled * inputs, 1, keepdims=True), (rows, 128))
    sums = exchange_sums(part, n, npeer, in_own, inn, n_s, n_r)
    for copy in sums:
        copy.wait()
    inner = inn[0]
    for k in range(1, 2 * X):
        inner = inner + inn[k]
    inverse = inv[...]
    slope = (inverse * inverse * inverse * (inner / D))[:, :1]
    out[...] = (inverse[:, :1] * scaled - inputs * slope).astype(BF16)
    for copy in started:
        copy.wait_send()


def scatter(zs, gn, emb, gain, inv):
    rows, width = emb.shape
    block = Y * rows
    vmem = pl.BlockSpec(memory_space=pltpu.VMEM)
    dma = pltpu.SemaphoreType.DMA
    half = zs // 2
    return pl.pallas_call(
        functools.partial(scatter_kernel, zs),
        out_shape=jax.ShapeDtypeStruct((rows, width), BF16),
        in_specs=[vmem] * 4,
        out_specs=vmem,
        scratch_shapes=[
            pltpu.VMEM((2, 2, half, block, width // 2), BF16),
            pltpu.VMEM((2, 2, half, block, width // 2), BF16),
            pltpu.VMEM((block, width), F32),
            pltpu.VMEM((Y, rows, width), F32),
            pltpu.VMEM((Y, rows, width), F32),
            pltpu.VMEM((rows, 128), F32),
            pltpu.VMEM((2 * X, rows, 128), F32),
            dma((2, 2, half)), dma((2, 2, half)),
            dma((Y,)), dma((Y,)),
            dma((2 * X,)), dma((2 * X,)),
        ],
        compiler_params=pltpu.CompilerParams(collective_id=2, has_side_effects=True),
        name="scatter",
    )(gn.reshape(zs, block, width), emb, gain, inv)


def rotary_tables(segment_ids):
    spots = jnp.arange(segment_ids.shape[0], dtype=jnp.int32)
    starts = jnp.sum((segment_ids[None, :] < segment_ids[:, None]).astype(jnp.int32), 1)
    position = (spots - starts).astype(F32)
    half = HDIM // 2
    frequency = jnp.exp(-(2.0 * jnp.arange(half, dtype=F32) / HDIM) * math.log(THETA))
    angle = position[:, None] * frequency[None, :]
    cosine, sine = jnp.cos(angle), jnp.sin(angle)
    return jnp.concatenate([cosine, cosine], 1), jnp.concatenate([-sine, sine], 1)


def swap(values):
    half = HDIM // 2
    return jnp.concatenate([values[:, half:], values[:, :half]], 1)


def dot(a, b, da, db):
    return lax.dot_general(a, b, (((da,), (db,)), ((), ())), preferred_element_type=F32)


def head_grads(q, k, v, g, allowed, scale):
    scores = jnp.where(allowed, dot(q, k, 1, 1) * scale, -1e30)
    raised = jnp.exp(scores - jnp.max(scores, 1, keepdims=True))
    attend = raised / jnp.sum(raised, 1, keepdims=True)
    grad_attend = dot(g, v, 1, 1)
    centre = jnp.sum(attend * grad_attend, 1, keepdims=True)
    grad_scores = (attend * (grad_attend - centre) * scale).astype(BF16)
    return (
        dot(grad_scores, k, 1, 0),
        dot(grad_scores, q, 0, 0),
        dot(attend.astype(BF16), g, 0, 0),
    )


def local(emb, norm_gain, query_weight, key_weight, value_weight, output_weight, segment_ids, cot):
    zs = lax.axis_size("wide") // Y
    total = segment_ids.shape[0]
    gain = norm_gain[None, :]
    e_all, c_all, kt, vt, inv = gather(zs, emb, gain, cot, key_weight.T, value_weight.T)
    width = emb.shape[1]
    e_all, c_all = e_all.reshape(total, width), c_all.reshape(total, width)
    kt, vt = kt.reshape(HDIM, width), vt.reshape(HDIM, width)
    cosine, sine = rotary_tables(segment_ids)
    heads = reduce_narrow(e_all, c_all, query_weight, kt, vt, output_weight, cosine, sine)
    q, k, v, g = (heads[:, i * HDIM : (i + 1) * HDIM] for i in range(4))
    spots = jnp.arange(total, dtype=jnp.int32)
    allowed = (segment_ids[:, None] == segment_ids[None, :]) & (spots[None, :] <= spots[:, None])
    gq, gk, gv = head_grads(q, k, v, g, allowed, HDIM ** (-0.5))
    gq = (gq * cosine - swap(gq) * sine).astype(BF16)
    gk = (gk * cosine - swap(gk) * sine).astype(BF16)
    gn = dot(gq, query_weight, 1, 1) + dot(gk, kt, 1, 0) + dot(gv.astype(BF16), vt, 1, 0)
    return scatter(zs, gn, emb, gain, inv)


def solution(mesh):
    return jax.shard_map(
        local,
        mesh=mesh,
        in_specs=(
            P("wide", "narrow"),
            P("narrow"),
            P("narrow", "wide"),
            P("narrow", "wide"),
            P("narrow", "wide"),
            P("wide", "narrow"),
            P(),
            P("wide", "narrow"),
        ),
        out_specs=P("wide", "narrow"),
        check_vma=False,
    )
```

```python
import functools
import math

import jax
import jax.numpy as jnp
from jax import lax
from jax.experimental import pallas as pl
from jax.experimental.pallas import tpu as pltpu
from jax.sharding import PartitionSpec as P

D = 8192
HDIM = 128
EPS = 1e-05
THETA = 500000.0
MESH = pl.DeviceIdType.MESH
Y = 4
X = 4
F32 = jnp.float32
BF16 = jnp.bfloat16


def remote(src, dst, send, recv, **where):
    return pltpu.make_async_remote_copy(
        src_ref=src, dst_ref=dst, send_sem=send, recv_sem=recv, device_id=where, device_id_type=MESH
    )


def meet(peers):
    barrier = pltpu.get_barrier_semaphore()
    for where in peers:
        pl.semaphore_signal(barrier, inc=1, device_id=where, device_id_type=MESH)
    pl.semaphore_wait(barrier, len(peers))


def places(zs):
    w, n = lax.axis_index("wide"), lax.axis_index("narrow")
    z, y = w // Y, w % Y
    ypeer = [z * Y + (y + k) % Y for k in range(Y)]
    up, down = ((z + 1) % zs) * Y + y, ((z + zs - 1) % zs) * Y + y
    npeer = [(n + k) % (2 * X) for k in range(2 * X)]
    return z, y, n, ypeer, up, down, npeer


def exchange_sums(value, n, npeer, own, slots, send, recv):
    own[...] = value
    slots[n] = value
    copies = [
        remote(own, slots.at[n], send.at[k], recv.at[k], narrow=npeer[k]) for k in range(1, len(npeer))
    ]
    for copy in copies:
        copy.start()
    return copies


def gather_kernel(
    zs, emb, gain, cot, kw, vw,
    e_out, c_out, k_out, v_out, inv_out,
    sq_own, sq, ey, cy, stage,
    sq_s, sq_r, y_s, y_r, wide_s, wide_r, thin_s, thin_r, spread_s, spread_r, kv_s, kv_r,
):
    z, y, n, ypeer, up, down, npeer = places(zs)
    rows, width = emb.shape
    half, wid = zs // 2, width // 2
    part = wid // Y
    outs = (c_out, e_out)
    twin = (z + 1 - 2 * (z % 2)) * Y + y
    meet([dict(narrow=npeer[k]) for k in range(1, 2 * X)]
         + [dict(wide=ypeer[k]) for k in range(1, Y)] + [dict(wide=up), dict(wide=down)])

    started = []

    def go(copy):
        copy.start()
        started.append(copy)
        return copy

    cot_y = [go(remote(cot, cy.at[y], y_s.at[0, k], y_r.at[0, k], wide=ypeer[k])) for k in range(1, Y)]
    x = emb[...].astype(F32)
    squares = jnp.broadcast_to(jnp.sum(x * x, 1, keepdims=True), (rows, 128))
    sums = exchange_sums(squares, n, npeer, sq_own, sq, sq_s, sq_r)
    slot = (z % 2) * Y + y
    pair = [
        go(remote(src, dst.at[slot], kv_s.at[i], kv_r.at[i], wide=twin))
        for i, (src, dst) in enumerate(((kw, k_out), (vw, v_out)))
    ]
    k_out[slot] = kw[...]
    v_out[slot] = vw[...]
    cy[y] = cot[...]

    def settle(copies, blocks, out):
        for copy in copies:
            copy.wait_recv()
        for j in range(Y):
            stage[rows * j : rows * (j + 1), :] = blocks[j].astype(F32)
        out[z] = stage[...].astype(BF16)

    def step(ring, view, sems, a, s):
        if s > 0:
            for way in range(2):
                if (way, a, s - 1) in ring:
                    ring[way, a, s - 1].wait_recv()
        for way in range(2):
            if s >= half or (s == half - 1 and a != way):
                continue
            here = view(outs[a], (z + zs - s) % zs if way == 0 else (z + s) % zs)
            ring[way, a, s] = go(
                remote(here, here, sems[0].at[way, a, s], sems[1].at[way, a, s], wide=(up, down)[way])
            )

    broad, thin = {}, {}

    def broad_step(a, s):
        step(broad, lambda ref, block: ref.at[block, :, 0:wid], (wide_s, wide_r), a, s)

    def lane(yy):
        return pl.ds(pl.multiple_of(wid + part * yy, 128), part)

    def thin_step(s):
        for a in range(2):
            step(thin, lambda ref, block: ref.at[block, :, lane(y)], (thin_s, thin_r), a, s)

    def y_send(i, j, here, k):
        return go(remote(here, here, spread_s.at[i, j], spread_r.at[i, j], wide=ypeer[k]))

    def spread(i, view):
        first = [y_send(i, j, view(j % 2, y), 1 if j < 2 else Y - 1) for j in range(4)]
        return [i, view, first]

    def relay(item):
        i, view, first = item
        first[0].wait_recv()
        first[3].wait_recv()
        item.append(y_send(i, 4, view(0, (y + Y - 1) % Y), 1))
        item.append(y_send(i, 5, view(1, (y + 1) % Y), Y - 1))

    def finish(item):
        item[2][1].wait_recv()
        item[2][2].wait_recv()
        item[3].wait_recv()
        item[4].wait_recv()

    def thin_view(block):
        return lambda a, yy: outs[a].at[block, :, lane(yy)]

    def kv_view(base):
        return lambda a, yy: (k_out, v_out)[a].at[base + yy]

    settle(cot_y, cy, c_out)
    broad_step(0, 0)
    for copy in sums:
        copy.wait()
    total = sq[0]
    for k in range(1, 2 * X):
        total = total + sq[k]
    inverse = lax.rsqrt(total / D + EPS)
    inv_out[...] = inverse
    ey[y] = (x * inverse[:, :1] * gain[...].astype(F32)).astype(BF16)
    emb_y = [go(remote(ey.at[y], ey.at[y], y_s.at[1, k], y_r.at[1, k], wide=ypeer[k])) for k in range(1, Y)]
    settle(emb_y, ey, e_out)
    count = 2 * half - 1
    items, relayed = [], 0

    def spread_after(s):
        if s < half - 1:
            items.append(spread(2 * s, thin_view((z + zs - s - 1) % zs)))
            items.append(spread(2 * s + 1, thin_view((z + s + 1) % zs)))
        else:
            items.append(spread(2 * s, thin_view((z + half) % zs)))

    for s in range(half):
        ready = len(items)
        thin_step(s)
        if s > 0:
            spread_after(s - 1)
            broad_step(0, s)
        broad_step(1, s)
        for item in items[relayed:ready]:
            relay(item)
        relayed = ready
        if s == 0:
            for copy in pair:
                copy.wait_recv()
            items.append(spread(count, kv_view((z % 2) * Y)))
            items.append(spread(count + 1, kv_view(Y - (z % 2) * Y)))
    thin_step(half)
    spread_after(half - 1)
    for item in items[relayed:]:
        relay(item)
    for item in items:
        finish(item)
    for a in range(2):
        broad[a, a, half - 1].wait_recv()
    for copy in started:
        copy.wait_send()


def gather(zs, emb, gain, cot, kw, vw):
    rows, width = emb.shape
    vmem = pl.BlockSpec(memory_space=pltpu.VMEM)
    block = Y * rows
    dma = pltpu.SemaphoreType.DMA
    return pl.pallas_call(
        functools.partial(gather_kernel, zs),
        out_shape=(
            jax.ShapeDtypeStruct((zs, block, width), BF16),
            jax.ShapeDtypeStruct((zs, block, width), BF16),
            jax.ShapeDtypeStruct((2 * Y,) + kw.shape, BF16),
            jax.ShapeDtypeStruct((2 * Y,) + vw.shape, BF16),
            jax.ShapeDtypeStruct((rows, 128), F32),
        ),
        in_specs=[vmem] * 5,
        out_specs=(vmem,) * 5,
        scratch_shapes=[
            pltpu.VMEM((rows, 128), F32),
            pltpu.VMEM((2 * X, rows, 128), F32),
            pltpu.VMEM((Y, rows, width), BF16),
            pltpu.VMEM((Y, rows, width), BF16),
            pltpu.VMEM((block, width), F32),
            dma((2 * X,)), dma((2 * X,)),
            dma((2, Y)), dma((2, Y)),
            dma((2, 2, zs // 2)), dma((2, 2, zs // 2)),
            dma((2, 2, zs // 2)), dma((2, 2, zs // 2)),
            dma((zs + 1, 6)), dma((zs + 1, 6)),
            dma((2,)), dma((2,)),
        ],
        compiler_params=pltpu.CompilerParams(collective_id=0, has_side_effects=True),
        name="gather",
    )(emb, gain, cot, kw, vw)


def reduce_kernel(
    e_all, c_all, qw, kt, vt, ow, cosine, sine, out,
    away, home, pbuf, sbuf, rbuf,
    p_s, p_r, x_s, x_r, gx_s, gx_r, gp_s, gp_r,
):
    n = lax.axis_index("narrow")
    x, core = n // 2, n % 2
    twin = x * 2 + 1 - core
    xs = [(x + k) % X for k in range(X)]
    meet([dict(narrow=twin)] + [dict(narrow=xs[k] * 2 + core) for k in (1, X - 1)])
    order = (2, 1, 3, 0)
    started = []

    def go(copy):
        copy.start()
        started.append(copy)
        return copy

    def project(side, into):
        e, c = e_all[side], c_all[side]
        for i, (rows, weight, over) in enumerate(((e, qw, 0), (e, kt, 1), (e, vt, 1), (c, ow, 1))):
            value = dot(rows, weight[...], 1, over)
            into[:, :, i * HDIM : (i + 1) * HDIM] = value.reshape(into.shape[:2] + (HDIM,))

    project(1 - core, away)
    first = {
        k: go(remote(away.at[xs[k]], pbuf.at[xs[k]], p_s.at[k], p_r.at[k], narrow=twin))
        for k in order
    }
    project(core, home)
    lo, hi = slice(0, 2 * HDIM), slice(2 * HDIM, 4 * HDIM)
    right, left = xs[1] * 2 + core, xs[X - 1] * 2 + core

    def pair_sum(k):
        first[k].wait_recv()
        return home[xs[k]] + pbuf[xs[k]]

    def hand(i, value, where):
        sbuf[i] = value
        return go(remote(sbuf.at[i], rbuf.at[i], x_s.at[i], x_r.at[i], narrow=where))

    value = pair_sum(2)
    chain_lo = hand(0, value[:, lo], right)
    chain_hi = hand(1, value[:, hi], left)
    value = pair_sum(1)
    near_hi = hand(2, value[:, hi], right)
    ahead = value[:, lo]
    value = pair_sum(3)
    near_lo = hand(3, value[:, lo], left)
    behind = value[:, hi]
    chain_lo.wait_recv()
    far_lo = hand(4, ahead + rbuf[0], right)
    chain_hi.wait_recv()
    far_hi = hand(5, behind + rbuf[1], left)
    value = pair_sum(0)
    near_lo.wait_recv()
    near_hi.wait_recv()
    total_lo = value[:, lo] + rbuf[3]
    total_hi = value[:, hi] + rbuf[2]
    far_lo.wait_recv()
    far_hi.wait_recv()
    total = jnp.concatenate([total_lo + rbuf[4], total_hi + rbuf[5]], 1)
    cos, sin = cosine[core, x], sine[core, x]
    for i in range(4):
        value = total[:, i * HDIM : (i + 1) * HDIM]
        if i < 2:
            value = value * cos + pltpu.roll(value, HDIM // 2, 1) * sin
        out[core, x, :, i * HDIM : (i + 1) * HDIM] = value.astype(BF16)
    mine = out.at[core, x]
    def give(i, here, where):
        return go(remote(here, here, gx_s.at[i], gx_r.at[i], narrow=where))

    given = [give(0, mine, right), give(1, mine, left)]
    shared = [go(remote(mine, mine, gp_s.at[0], gp_r.at[0], narrow=twin))]

    def share(k):
        block = out.at[core, xs[k]]
        shared.append(go(remote(block, block, gp_s.at[k], gp_r.at[k], narrow=twin)))

    given[0].wait_recv()
    far = [give(2, out.at[core, xs[3], :, lo], right)]
    share(3)
    given[1].wait_recv()
    far.append(give(3, out.at[core, xs[1], :, hi], left))
    share(1)
    for copy in far:
        copy.wait_recv()
    share(2)
    for copy in shared:
        copy.wait_recv()
    for copy in started:
        copy.wait_send()


def reduce_narrow(e_all, c_all, qw, kt, vt, ow, cosine, sine):
    tokens, cols = cosine.shape[0], 4 * HDIM
    chunk = tokens // (2 * X)
    vmem = pl.BlockSpec(memory_space=pltpu.VMEM)
    dma = pltpu.SemaphoreType.DMA
    out = pl.pallas_call(
        reduce_kernel,
        out_shape=jax.ShapeDtypeStruct((2, X, chunk, cols), BF16),
        in_specs=[vmem] * 8,
        out_specs=vmem,
        scratch_shapes=[pltpu.VMEM((X, chunk, cols), F32)] * 3
        + [pltpu.VMEM((6, chunk, cols // 2), F32)] * 2
        + [dma((X,))] * 2 + [dma((6,))] * 2 + [dma((X,))] * 4,
        compiler_params=pltpu.CompilerParams(collective_id=1, has_side_effects=True),
        name="reduce",
    )(
        e_all.reshape(2, X * chunk, -1),
        c_all.reshape(2, X * chunk, -1),
        qw, kt, vt, ow,
        cosine.reshape(2, X, chunk, HDIM),
        sine.reshape(2, X, chunk, HDIM),
    )
    return out.reshape(tokens, cols)


def scatter_kernel(
    zs, gq, gk, gv, qw, kt, vt, emb, gain, inv, out,
    gn, sbuf, rbuf, stage, ysend, yrecv, in_own, inn,
    z_s, z_r, y_s, y_r, n_s, n_r,
):
    z, y, n, ypeer, up, down, npeer = places(zs)
    rows, width = emb.shape
    half = zs // 2
    meet([dict(narrow=npeer[k]) for k in range(1, 2 * X)]
         + [dict(wide=ypeer[k]) for k in range(1, Y)] + [dict(wide=up), dict(wide=down)])
    started = []

    def go(copy):
        copy.start()
        started.append(copy)
        return copy

    chain = {}
    groups = rbuf.shape[1]
    wid = width // groups
    lanes = [slice(h * wid, (h + 1) * wid) for h in range(groups)]
    for s in range(half):
        for h in range(groups):
            cut = lanes[h]
            if s == 0:
                value = dot(gq[...], qw[cut, :], 1, 1) + dot(gk[...], kt[:, cut], 1, 0)
                value = value + dot(gv[...], vt[:, cut], 1, 0)
                gn[:, :, cut] = value.reshape(zs, Y * rows, wid)
            for way in range(2):
                length = half if h % 2 == way else half - 1
                if s >= length:
                    continue
                far = length - s
                block = (z + far) % zs if way == 0 else (z + zs - far) % zs
                value = gn[block, :, cut]
                if s:
                    chain[way, h].wait_recv()
                    value = value + rbuf[way, h, s - 1].astype(F32)
                sbuf[way, h, s] = value.astype(BF16)
                chain[way, h] = go(
                    remote(
                        sbuf.at[way, h, s], rbuf.at[way, h, s], z_s.at[way, h, s], z_r.at[way, h, s],
                        wide=(up, down)[way],
                    )
                )
    for h in range(groups):
        value = gn[z, :, lanes[h]]
        for way in range(2):
            length = half if h % 2 == way else half - 1
            chain[way, h].wait_recv()
            value = value + rbuf[way, h, length - 1].astype(F32)
        stage[:, lanes[h]] = value
    for j in range(Y):
        ysend[j] = stage[rows * j : rows * (j + 1), :]
    yrecv[y] = ysend[y]
    last = [
        go(remote(ysend.at[(y + k) % Y], yrecv.at[y], y_s.at[k], y_r.at[k], wide=ypeer[k]))
        for k in range(1, Y)
    ]
    for copy in last:
        copy.wait_recv()
    scaled = (yrecv[0] + yrecv[1] + yrecv[2] + yrecv[3]) * gain[...].astype(F32)
    inputs = emb[...].astype(F32)
    part = jnp.broadcast_to(jnp.sum(scaled * inputs, 1, keepdims=True), (rows, 128))
    sums = exchange_sums(part, n, npeer, in_own, inn, n_s, n_r)
    for copy in sums:
        copy.wait()
    inner = inn[0]
    for k in range(1, 2 * X):
        inner = inner + inn[k]
    inverse = inv[...]
    slope = (inverse * inverse * inverse * (inner / D))[:, :1]
    out[...] = (inverse[:, :1] * scaled - inputs * slope).astype(BF16)
    for copy in started:
        copy.wait_send()


def scatter(zs, gq, gk, gv, qw, kt, vt, emb, gain, inv):
    rows, width = emb.shape
    block = Y * rows
    vmem = pl.BlockSpec(memory_space=pltpu.VMEM)
    dma = pltpu.SemaphoreType.DMA
    half = zs // 2
    return pl.pallas_call(
        functools.partial(scatter_kernel, zs),
        out_shape=jax.ShapeDtypeStruct((rows, width), BF16),
        in_specs=[vmem] * 9,
        out_specs=vmem,
        scratch_shapes=[
            pltpu.VMEM((zs, block, width), F32),
            pltpu.VMEM((2, 4, half, block, width // 4), BF16),
            pltpu.VMEM((2, 4, half, block, width // 4), BF16),
            pltpu.VMEM((block, width), F32),
            pltpu.VMEM((Y, rows, width), F32),
            pltpu.VMEM((Y, rows, width), F32),
            pltpu.VMEM((rows, 128), F32),
            pltpu.VMEM((2 * X, rows, 128), F32),
            dma((2, 4, half)), dma((2, 4, half)),
            dma((Y,)), dma((Y,)),
            dma((2 * X,)), dma((2 * X,)),
        ],
        compiler_params=pltpu.CompilerParams(collective_id=2, has_side_effects=True),
        name="scatter",
    )(gq, gk, gv, qw, kt, vt, emb, gain, inv)


def rotary_tables(segment_ids):
    spots = jnp.arange(segment_ids.shape[0], dtype=jnp.int32)
    starts = jnp.sum((segment_ids[None, :] < segment_ids[:, None]).astype(jnp.int32), 1)
    position = (spots - starts).astype(F32)
    half = HDIM // 2
    frequency = jnp.exp(-(2.0 * jnp.arange(half, dtype=F32) / HDIM) * math.log(THETA))
    angle = position[:, None] * frequency[None, :]
    cosine, sine = jnp.cos(angle), jnp.sin(angle)
    return jnp.concatenate([cosine, cosine], 1), jnp.concatenate([-sine, sine], 1)


def swap(values):
    half = HDIM // 2
    return jnp.concatenate([values[:, half:], values[:, :half]], 1)


def dot(a, b, da, db):
    return lax.dot_general(a, b, (((da,), (db,)), ((), ())), preferred_element_type=F32)


def head_grads(q, k, v, g, allowed, scale):
    scores = jnp.where(allowed, dot(q, k, 1, 1) * scale, -1e30)
    raised = jnp.exp(scores - jnp.max(scores, 1, keepdims=True))
    attend = raised / jnp.sum(raised, 1, keepdims=True)
    grad_attend = dot(g, v, 1, 1)
    centre = jnp.sum(attend * grad_attend, 1, keepdims=True)
    grad_scores = (attend * (grad_attend - centre) * scale).astype(BF16)
    return (
        dot(grad_scores, k, 1, 0),
        dot(grad_scores, q, 0, 0),
        dot(attend.astype(BF16), g, 0, 0),
    )


def local(emb, norm_gain, query_weight, key_weight, value_weight, output_weight, segment_ids, cot):
    zs = lax.axis_size("wide") // Y
    total = segment_ids.shape[0]
    gain = norm_gain[None, :]
    e_all, c_all, kt, vt, inv = gather(zs, emb, gain, cot, key_weight.T, value_weight.T)
    width = emb.shape[1]
    e_all, c_all = e_all.reshape(total, width), c_all.reshape(total, width)
    kt, vt = kt.reshape(HDIM, width), vt.reshape(HDIM, width)
    cosine, sine = rotary_tables(segment_ids)
    heads = reduce_narrow(e_all, c_all, query_weight, kt, vt, output_weight, cosine, sine)
    q, k, v, g = (heads[:, i * HDIM : (i + 1) * HDIM] for i in range(4))
    spots = jnp.arange(total, dtype=jnp.int32)
    allowed = (segment_ids[:, None] == segment_ids[None, :]) & (spots[None, :] <= spots[:, None])
    gq, gk, gv = head_grads(q, k, v, g, allowed, HDIM ** (-0.5))
    gq = (gq * cosine - swap(gq) * sine).astype(BF16)
    gk = (gk * cosine - swap(gk) * sine).astype(BF16)
    return scatter(zs, gq, gk, gv.astype(BF16), query_weight, kt, vt, emb, gain, inv)


def solution(mesh):
    return jax.shard_map(
        local,
        mesh=mesh,
        in_specs=(
            P("wide", "narrow"),
            P("narrow"),
            P("narrow", "wide"),
            P("narrow", "wide"),
            P("narrow", "wide"),
            P("wide", "narrow"),
            P(),
            P("wide", "narrow"),
        ),
        out_specs=P("wide", "narrow"),
        check_vma=False,
    )
```

```python
import functools
import math

import jax
import jax.numpy as jnp
from jax import lax
from jax.experimental import pallas as pl
from jax.experimental.pallas import tpu as pltpu
from jax.sharding import PartitionSpec as P

D = 8192
HDIM = 128
EPS = 1e-05
THETA = 500000.0
MESH = pl.DeviceIdType.MESH
Y = 4
X = 4
F32 = jnp.float32
BF16 = jnp.bfloat16


def remote(src, dst, send, recv, **where):
    return pltpu.make_async_remote_copy(
        src_ref=src, dst_ref=dst, send_sem=send, recv_sem=recv, device_id=where, device_id_type=MESH
    )


def meet(peers):
    barrier = pltpu.get_barrier_semaphore()
    for where in peers:
        pl.semaphore_signal(barrier, inc=1, device_id=where, device_id_type=MESH)
    pl.semaphore_wait(barrier, len(peers))


def places(zs):
    w, n = lax.axis_index("wide"), lax.axis_index("narrow")
    z, y = w // Y, w % Y
    ypeer = [z * Y + (y + k) % Y for k in range(Y)]
    up, down = ((z + 1) % zs) * Y + y, ((z + zs - 1) % zs) * Y + y
    npeer = [(n + k) % (2 * X) for k in range(2 * X)]
    return z, y, n, ypeer, up, down, npeer


def exchange_sums(value, n, npeer, own, slots, send, recv):
    own[...] = value
    slots[n] = value
    copies = [
        remote(own, slots.at[n], send.at[k], recv.at[k], narrow=npeer[k]) for k in range(1, len(npeer))
    ]
    for copy in copies:
        copy.start()
    return copies


def gather_kernel(
    zs, emb, gain, cot, kw, vw,
    e_out, c_out, k_out, v_out, inv_out,
    sq_own, sq, ey, cy, stage,
    sq_s, sq_r, y_s, y_r, wide_s, wide_r, thin_s, thin_r, spread_s, spread_r, kv_s, kv_r,
):
    z, y, n, ypeer, up, down, npeer = places(zs)
    rows, width = emb.shape
    half, wid = zs // 2, width // 2
    part = wid // Y
    outs = (c_out, e_out)
    twin = (z + 1 - 2 * (z % 2)) * Y + y
    meet([dict(narrow=npeer[k]) for k in range(1, 2 * X)]
         + [dict(wide=ypeer[k]) for k in range(1, Y)] + [dict(wide=up), dict(wide=down)])

    started = []

    def go(copy):
        copy.start()
        started.append(copy)
        return copy

    cot_y = [go(remote(cot, cy.at[y], y_s.at[0, k], y_r.at[0, k], wide=ypeer[k])) for k in range(1, Y)]
    x = emb[...].astype(F32)
    squares = jnp.broadcast_to(jnp.sum(x * x, 1, keepdims=True), (rows, 128))
    sums = exchange_sums(squares, n, npeer, sq_own, sq, sq_s, sq_r)
    slot = (z % 2) * Y + y
    pair = [
        go(remote(src, dst.at[slot], kv_s.at[i], kv_r.at[i], wide=twin))
        for i, (src, dst) in enumerate(((kw, k_out), (vw, v_out)))
    ]
    k_out[slot] = kw[...]
    v_out[slot] = vw[...]
    cy[y] = cot[...]

    def settle(copies, blocks, out):
        for copy in copies:
            copy.wait_recv()
        for j in range(Y):
            stage[rows * j : rows * (j + 1), :] = blocks[j].astype(F32)
        out[z] = stage[...].astype(BF16)

    def step(ring, view, sems, a, s):
        if s > 0:
            for way in range(2):
                if (way, a, s - 1) in ring:
                    ring[way, a, s - 1].wait_recv()
        for way in range(2):
            if s >= half or (s == half - 1 and a != way):
                continue
            here = view(outs[a], (z + zs - s) % zs if way == 0 else (z + s) % zs)
            ring[way, a, s] = go(
                remote(here, here, sems[0].at[way, a, s], sems[1].at[way, a, s], wide=(up, down)[way])
            )

    broad, thin = {}, {}

    def broad_step(a, s):
        step(broad, lambda ref, block: ref.at[block, :, 0:wid], (wide_s, wide_r), a, s)

    def lane(yy):
        return pl.ds(pl.multiple_of(wid + part * yy, 128), part)

    def thin_step(s):
        for a in range(2):
            step(thin, lambda ref, block: ref.at[block, :, lane(y)], (thin_s, thin_r), a, s)

    def y_send(i, j, here, k):
        return go(remote(here, here, spread_s.at[i, j], spread_r.at[i, j], wide=ypeer[k]))

    def spread(i, view):
        first = [y_send(i, j, view(j % 2, y), 1 if j < 2 else Y - 1) for j in range(4)]
        return [i, view, first]

    def relay(item):
        i, view, first = item
        first[0].wait_recv()
        first[3].wait_recv()
        item.append(y_send(i, 4, view(0, (y + Y - 1) % Y), 1))
        item.append(y_send(i, 5, view(1, (y + 1) % Y), Y - 1))

    def finish(item):
        item[2][1].wait_recv()
        item[2][2].wait_recv()
        item[3].wait_recv()
        item[4].wait_recv()

    def thin_view(block):
        return lambda a, yy: outs[a].at[block, :, lane(yy)]

    def kv_view(base):
        return lambda a, yy: (k_out, v_out)[a].at[base + yy]

    settle(cot_y, cy, c_out)
    broad_step(0, 0)
    for copy in sums:
        copy.wait()
    total = sq[0]
    for k in range(1, 2 * X):
        total = total + sq[k]
    inverse = lax.rsqrt(total / D + EPS)
    inv_out[...] = inverse
    ey[y] = (x * inverse[:, :1] * gain[...].astype(F32)).astype(BF16)
    emb_y = [go(remote(ey.at[y], ey.at[y], y_s.at[1, k], y_r.at[1, k], wide=ypeer[k])) for k in range(1, Y)]
    settle(emb_y, ey, e_out)
    count = 2 * half - 1
    items, relayed = [], 0

    def spread_after(s):
        if s < half - 1:
            items.append(spread(2 * s, thin_view((z + zs - s - 1) % zs)))
            items.append(spread(2 * s + 1, thin_view((z + s + 1) % zs)))
        else:
            items.append(spread(2 * s, thin_view((z + half) % zs)))

    for s in range(half):
        ready = len(items)
        thin_step(s)
        if s > 0:
            spread_after(s - 1)
            broad_step(0, s)
        broad_step(1, s)
        for item in items[relayed:ready]:
            relay(item)
        relayed = ready
        if s == 0:
            for copy in pair:
                copy.wait_recv()
            items.append(spread(count, kv_view((z % 2) * Y)))
            items.append(spread(count + 1, kv_view(Y - (z % 2) * Y)))
    thin_step(half)
    spread_after(half - 1)
    for item in items[relayed:]:
        relay(item)
    for item in items:
        finish(item)
    for a in range(2):
        broad[a, a, half - 1].wait_recv()
    for copy in started:
        copy.wait_send()


def reduce_kernel(
    e_all, c_all, qw, kt, vt, ow, cosine, sine, out,
    away, home, pbuf, sbuf, rbuf,
    p_s, p_r, x_s, x_r, gx_s, gx_r, gp_s, gp_r,
):
    n = lax.axis_index("narrow")
    x, core = n // 2, n % 2
    twin = x * 2 + 1 - core
    xs = [(x + k) % X for k in range(X)]
    order = (2, 1, 3, 0)
    started = []

    def go(copy):
        copy.start()
        started.append(copy)
        return copy

    def project(side, into):
        blocks, width = e_all.shape[0] // 2, e_all.shape[2]
        part = pl.ds(side * blocks, blocks)
        e, c = (ref[part].reshape(-1, width) for ref in (e_all, c_all))
        keys, values = (ref[...].reshape(HDIM, width) for ref in (kt, vt))
        given = ((e, qw[...], 0), (e, keys, 1), (e, values, 1), (c, ow[...], 1))
        for i, (rows, weight, over) in enumerate(given):
            value = dot(rows, weight, 1, over)
            into[:, :, i * HDIM : (i + 1) * HDIM] = value.reshape(into.shape[:2] + (HDIM,))

    project(1 - core, away)
    first = {
        k: go(remote(away.at[xs[k]], pbuf.at[xs[k]], p_s.at[k], p_r.at[k], narrow=twin))
        for k in order
    }
    project(core, home)
    lo, hi = slice(0, 2 * HDIM), slice(2 * HDIM, 4 * HDIM)
    right, left = xs[1] * 2 + core, xs[X - 1] * 2 + core

    def pair_sum(k):
        first[k].wait_recv()
        return home[xs[k]] + pbuf[xs[k]]

    def hand(i, value, where):
        sbuf[i] = value
        return go(remote(sbuf.at[i], rbuf.at[i], x_s.at[i], x_r.at[i], narrow=where))

    value = pair_sum(2)
    chain_lo = hand(0, value[:, lo], right)
    chain_hi = hand(1, value[:, hi], left)
    value = pair_sum(1)
    near_hi = hand(2, value[:, hi], right)
    ahead = value[:, lo]
    value = pair_sum(3)
    near_lo = hand(3, value[:, lo], left)
    behind = value[:, hi]
    chain_lo.wait_recv()
    far_lo = hand(4, ahead + rbuf[0], right)
    chain_hi.wait_recv()
    far_hi = hand(5, behind + rbuf[1], left)
    value = pair_sum(0)
    near_lo.wait_recv()
    near_hi.wait_recv()
    total_lo = value[:, lo] + rbuf[3]
    total_hi = value[:, hi] + rbuf[2]
    far_lo.wait_recv()
    far_hi.wait_recv()
    total = jnp.concatenate([total_lo + rbuf[4], total_hi + rbuf[5]], 1)
    cos, sin = cosine[core, x], sine[core, x]
    for i in range(4):
        value = total[:, i * HDIM : (i + 1) * HDIM]
        if i < 2:
            value = value * cos + pltpu.roll(value, HDIM // 2, 1) * sin
        out[core, x, :, i * HDIM : (i + 1) * HDIM] = value.astype(BF16)
    mine = out.at[core, x]
    def give(i, here, where):
        return go(remote(here, here, gx_s.at[i], gx_r.at[i], narrow=where))

    given = [give(0, mine, right), give(1, mine, left)]
    shared = [go(remote(mine, mine, gp_s.at[0], gp_r.at[0], narrow=twin))]

    def share(k):
        block = out.at[core, xs[k]]
        shared.append(go(remote(block, block, gp_s.at[k], gp_r.at[k], narrow=twin)))

    given[0].wait_recv()
    far = [give(2, out.at[core, xs[3], :, lo], right)]
    share(3)
    given[1].wait_recv()
    far.append(give(3, out.at[core, xs[1], :, hi], left))
    share(1)
    for copy in far:
        copy.wait_recv()
    share(2)
    for copy in shared:
        copy.wait_recv()
    for copy in started:
        copy.wait_send()


def front_kernel(
    zs, emb, gain, cot, kw, vw, qw, ow, cosine, sine,
    out, k_out, v_out, inv_out,
    e_all, c_all, *scratch,
):
    gather_kernel(zs, emb, gain, cot, kw, vw, e_all, c_all, k_out, v_out, inv_out, *scratch[:17])
    reduce_kernel(e_all, c_all, qw, k_out, v_out, ow, cosine, sine, out, *scratch[17:])


def front(zs, emb, gain, cot, kw, vw, qw, ow, cosine, sine):
    rows, width = emb.shape
    block = Y * rows
    tokens, cols = zs * block, 4 * HDIM
    chunk = tokens // (2 * X)
    vmem = pl.BlockSpec(memory_space=pltpu.VMEM)
    dma = pltpu.SemaphoreType.DMA
    return pl.pallas_call(
        functools.partial(front_kernel, zs),
        out_shape=(
            jax.ShapeDtypeStruct((2, X, chunk, cols), BF16),
            jax.ShapeDtypeStruct((2 * Y,) + kw.shape, BF16),
            jax.ShapeDtypeStruct((2 * Y,) + vw.shape, BF16),
            jax.ShapeDtypeStruct((rows, 128), F32),
        ),
        in_specs=[vmem] * 9,
        out_specs=(vmem,) * 4,
        scratch_shapes=[
            pltpu.VMEM((zs, block, width), BF16),
            pltpu.VMEM((zs, block, width), BF16),
            pltpu.VMEM((rows, 128), F32),
            pltpu.VMEM((2 * X, rows, 128), F32),
            pltpu.VMEM((Y, rows, width), BF16),
            pltpu.VMEM((Y, rows, width), BF16),
            pltpu.VMEM((block, width), F32),
            dma((2 * X,)), dma((2 * X,)),
            dma((2, Y)), dma((2, Y)),
            dma((2, 2, zs // 2)), dma((2, 2, zs // 2)),
            dma((2, 2, zs // 2)), dma((2, 2, zs // 2)),
            dma((zs + 1, 6)), dma((zs + 1, 6)),
            dma((2,)), dma((2,)),
        ]
        + [pltpu.VMEM((X, chunk, cols), F32)] * 3
        + [pltpu.VMEM((6, chunk, cols // 2), F32)] * 2
        + [dma((X,))] * 2 + [dma((6,))] * 2 + [dma((X,))] * 4,
        compiler_params=pltpu.CompilerParams(collective_id=0, has_side_effects=True),
        name="front",
    )(
        emb, gain, cot, kw, vw, qw, ow,
        cosine.reshape(2, X, chunk, HDIM),
        sine.reshape(2, X, chunk, HDIM),
    )


def scatter_kernel(
    zs, gq, gk, gv, qw, kt, vt, emb, gain, inv, out,
    gn, sbuf, rbuf, stage, ysend, yrecv, in_own, inn,
    z_s, z_r, y_s, y_r, n_s, n_r,
):
    z, y, n, ypeer, up, down, npeer = places(zs)
    rows, width = emb.shape
    half = zs // 2
    meet([dict(narrow=npeer[k]) for k in range(1, 2 * X)]
         + [dict(wide=ypeer[k]) for k in range(1, Y)] + [dict(wide=up), dict(wide=down)])
    started = []

    def go(copy):
        copy.start()
        started.append(copy)
        return copy

    chain = {}
    groups = rbuf.shape[1]
    wid = width // groups
    lanes = [slice(h * wid, (h + 1) * wid) for h in range(groups)]
    for s in range(half):
        for h in range(groups):
            cut = lanes[h]
            if s == 0:
                value = dot(gq[...], qw[cut, :], 1, 1) + dot(gk[...], kt[:, cut], 1, 0)
                value = value + dot(gv[...], vt[:, cut], 1, 0)
                gn[:, :, cut] = value.reshape(zs, Y * rows, wid)
            for way in range(2):
                length = half if h % 2 == way else half - 1
                if s >= length:
                    continue
                far = length - s
                block = (z + far) % zs if way == 0 else (z + zs - far) % zs
                value = gn[block, :, cut]
                if s:
                    chain[way, h].wait_recv()
                    value = value + rbuf[way, h, s - 1].astype(F32)
                sbuf[way, h, s] = value.astype(BF16)
                chain[way, h] = go(
                    remote(
                        sbuf.at[way, h, s], rbuf.at[way, h, s], z_s.at[way, h, s], z_r.at[way, h, s],
                        wide=(up, down)[way],
                    )
                )
    for h in range(groups):
        value = gn[z, :, lanes[h]]
        for way in range(2):
            length = half if h % 2 == way else half - 1
            chain[way, h].wait_recv()
            value = value + rbuf[way, h, length - 1].astype(F32)
        stage[:, lanes[h]] = value
    for j in range(Y):
        ysend[j] = stage[rows * j : rows * (j + 1), :]
    yrecv[y] = ysend[y]
    last = [
        go(remote(ysend.at[(y + k) % Y], yrecv.at[y], y_s.at[k], y_r.at[k], wide=ypeer[k]))
        for k in range(1, Y)
    ]
    for copy in last:
        copy.wait_recv()
    scaled = (yrecv[0] + yrecv[1] + yrecv[2] + yrecv[3]) * gain[...].astype(F32)
    inputs = emb[...].astype(F32)
    part = jnp.broadcast_to(jnp.sum(scaled * inputs, 1, keepdims=True), (rows, 128))
    sums = exchange_sums(part, n, npeer, in_own, inn, n_s, n_r)
    for copy in sums:
        copy.wait()
    inner = inn[0]
    for k in range(1, 2 * X):
        inner = inner + inn[k]
    inverse = inv[...]
    slope = (inverse * inverse * inverse * (inner / D))[:, :1]
    out[...] = (inverse[:, :1] * scaled - inputs * slope).astype(BF16)
    for copy in started:
        copy.wait_send()


def scatter(zs, gq, gk, gv, qw, kt, vt, emb, gain, inv):
    rows, width = emb.shape
    block = Y * rows
    vmem = pl.BlockSpec(memory_space=pltpu.VMEM)
    dma = pltpu.SemaphoreType.DMA
    half = zs // 2
    return pl.pallas_call(
        functools.partial(scatter_kernel, zs),
        out_shape=jax.ShapeDtypeStruct((rows, width), BF16),
        in_specs=[vmem] * 9,
        out_specs=vmem,
        scratch_shapes=[
            pltpu.VMEM((zs, block, width), F32),
            pltpu.VMEM((2, 4, half, block, width // 4), BF16),
            pltpu.VMEM((2, 4, half, block, width // 4), BF16),
            pltpu.VMEM((block, width), F32),
            pltpu.VMEM((Y, rows, width), F32),
            pltpu.VMEM((Y, rows, width), F32),
            pltpu.VMEM((rows, 128), F32),
            pltpu.VMEM((2 * X, rows, 128), F32),
            dma((2, 4, half)), dma((2, 4, half)),
            dma((Y,)), dma((Y,)),
            dma((2 * X,)), dma((2 * X,)),
        ],
        compiler_params=pltpu.CompilerParams(collective_id=2, has_side_effects=True),
        name="scatter",
    )(gq, gk, gv, qw, kt, vt, emb, gain, inv)


def rotary_tables(segment_ids):
    spots = jnp.arange(segment_ids.shape[0], dtype=jnp.int32)
    starts = jnp.sum((segment_ids[None, :] < segment_ids[:, None]).astype(jnp.int32), 1)
    position = (spots - starts).astype(F32)
    half = HDIM // 2
    frequency = jnp.exp(-(2.0 * jnp.arange(half, dtype=F32) / HDIM) * math.log(THETA))
    angle = position[:, None] * frequency[None, :]
    cosine, sine = jnp.cos(angle), jnp.sin(angle)
    return jnp.concatenate([cosine, cosine], 1), jnp.concatenate([-sine, sine], 1)


def swap(values):
    half = HDIM // 2
    return jnp.concatenate([values[:, half:], values[:, :half]], 1)


def dot(a, b, da, db):
    return lax.dot_general(a, b, (((da,), (db,)), ((), ())), preferred_element_type=F32)


def head_grads(q, k, v, g, allowed, scale):
    scores = jnp.where(allowed, dot(q, k, 1, 1) * scale, -1e30)
    raised = jnp.exp(scores - jnp.max(scores, 1, keepdims=True))
    attend = raised / jnp.sum(raised, 1, keepdims=True)
    grad_attend = dot(g, v, 1, 1)
    centre = jnp.sum(attend * grad_attend, 1, keepdims=True)
    grad_scores = (attend * (grad_attend - centre) * scale).astype(BF16)
    return (
        dot(grad_scores, k, 1, 0),
        dot(grad_scores, q, 0, 0),
        dot(attend.astype(BF16), g, 0, 0),
    )


def local(emb, norm_gain, query_weight, key_weight, value_weight, output_weight, segment_ids, cot):
    zs = lax.axis_size("wide") // Y
    total = segment_ids.shape[0]
    gain = norm_gain[None, :]
    width = emb.shape[1]
    cosine, sine = rotary_tables(segment_ids)
    heads, kt, vt, inv = front(
        zs, emb, gain, cot, key_weight.T, value_weight.T, query_weight, output_weight, cosine, sine
    )
    heads = heads.reshape(total, 4 * HDIM)
    kt, vt = kt.reshape(HDIM, width), vt.reshape(HDIM, width)
    q, k, v, g = (heads[:, i * HDIM : (i + 1) * HDIM] for i in range(4))
    spots = jnp.arange(total, dtype=jnp.int32)
    allowed = (segment_ids[:, None] == segment_ids[None, :]) & (spots[None, :] <= spots[:, None])
    gq, gk, gv = head_grads(q, k, v, g, allowed, HDIM ** (-0.5))
    gq = (gq * cosine - swap(gq) * sine).astype(BF16)
    gk = (gk * cosine - swap(gk) * sine).astype(BF16)
    return scatter(zs, gq, gk, gv.astype(BF16), query_weight, kt, vt, emb, gain, inv)


def solution(mesh):
    return jax.shard_map(
        local,
        mesh=mesh,
        in_specs=(
            P("wide", "narrow"),
            P("narrow"),
            P("narrow", "wide"),
            P("narrow", "wide"),
            P("narrow", "wide"),
            P("wide", "narrow"),
            P(),
            P("wide", "narrow"),
        ),
        out_specs=P("wide", "narrow"),
        check_vma=False,
    )
```

```python
import functools
import math

import jax
import jax.numpy as jnp
from jax import lax
from jax.experimental import pallas as pl
from jax.experimental.pallas import tpu as pltpu
from jax.sharding import PartitionSpec as P

D = 8192
HDIM = 128
EPS = 1e-05
THETA = 500000.0
MESH = pl.DeviceIdType.MESH
Y = 4
X = 4
F32 = jnp.float32
BF16 = jnp.bfloat16


def remote(src, dst, send, recv, **where):
    return pltpu.make_async_remote_copy(
        src_ref=src, dst_ref=dst, send_sem=send, recv_sem=recv, device_id=where, device_id_type=MESH
    )


def meet(peers):
    barrier = pltpu.get_barrier_semaphore()
    for where in peers:
        pl.semaphore_signal(barrier, inc=1, device_id=where, device_id_type=MESH)
    pl.semaphore_wait(barrier, len(peers))


def places(zs):
    w, n = lax.axis_index("wide"), lax.axis_index("narrow")
    z, y = w // Y, w % Y
    ypeer = [z * Y + (y + k) % Y for k in range(Y)]
    up, down = ((z + 1) % zs) * Y + y, ((z + zs - 1) % zs) * Y + y
    npeer = [(n + k) % (2 * X) for k in range(2 * X)]
    return z, y, n, ypeer, up, down, npeer


def exchange_sums(value, n, npeer, own, slots, send, recv):
    own[...] = value
    slots[n] = value
    copies = [
        remote(own, slots.at[n], send.at[k], recv.at[k], narrow=npeer[k]) for k in range(1, len(npeer))
    ]
    for copy in copies:
        copy.start()
    return copies


def gather_kernel(
    zs, emb, gain, cot, kw, vw,
    e_out, c_out, k_out, v_out, inv_out,
    sq_own, sq, ey, cy, stage,
    sq_s, sq_r, y_s, y_r, wide_s, wide_r, thin_s, thin_r, spread_s, spread_r, kv_s, kv_r,
):
    z, y, n, ypeer, up, down, npeer = places(zs)
    rows, width = emb.shape
    half, wid = zs // 2, width // 2
    part = wid // Y
    outs = (c_out, e_out)
    twin = (z + 1 - 2 * (z % 2)) * Y + y
    meet([dict(narrow=npeer[k]) for k in range(1, 2 * X)]
         + [dict(wide=ypeer[k]) for k in range(1, Y)] + [dict(wide=up), dict(wide=down)])

    started = []

    def go(copy):
        copy.start()
        started.append(copy)
        return copy

    cot_y = [go(remote(cot, cy.at[y], y_s.at[0, k], y_r.at[0, k], wide=ypeer[k])) for k in range(1, Y)]
    x = emb[...].astype(F32)
    squares = jnp.broadcast_to(jnp.sum(x * x, 1, keepdims=True), (rows, 128))
    sums = exchange_sums(squares, n, npeer, sq_own, sq, sq_s, sq_r)
    slot = (z % 2) * Y + y
    pair = [
        go(remote(src, dst.at[slot], kv_s.at[i], kv_r.at[i], wide=twin))
        for i, (src, dst) in enumerate(((kw, k_out), (vw, v_out)))
    ]
    k_out[slot] = kw[...]
    v_out[slot] = vw[...]
    cy[y] = cot[...]

    def settle(copies, blocks, out):
        for copy in copies:
            copy.wait_recv()
        for j in range(Y):
            stage[rows * j : rows * (j + 1), :] = blocks[j].astype(F32)
        out[z] = stage[...].astype(BF16)

    def step(ring, view, sems, a, s):
        if s > 0:
            for way in range(2):
                if (way, a, s - 1) in ring:
                    ring[way, a, s - 1].wait_recv()
        for way in range(2):
            if s >= half or (s == half - 1 and a != way):
                continue
            here = view(outs[a], (z + zs - s) % zs if way == 0 else (z + s) % zs)
            ring[way, a, s] = go(
                remote(here, here, sems[0].at[way, a, s], sems[1].at[way, a, s], wide=(up, down)[way])
            )

    broad, thin = {}, {}

    def broad_step(a, s):
        step(broad, lambda ref, block: ref.at[block, :, 0:wid], (wide_s, wide_r), a, s)

    def lane(yy):
        return pl.ds(pl.multiple_of(wid + part * yy, 128), part)

    def thin_step(s):
        for a in range(2):
            step(thin, lambda ref, block: ref.at[block, :, lane(y)], (thin_s, thin_r), a, s)

    def y_send(i, j, here, k):
        return go(remote(here, here, spread_s.at[i, j], spread_r.at[i, j], wide=ypeer[k]))

    def spread(i, view):
        first = [y_send(i, j, view(j % 2, y), 1 if j < 2 else Y - 1) for j in range(4)]
        return [i, view, first]

    def relay(item):
        i, view, first = item
        first[0].wait_recv()
        first[3].wait_recv()
        item.append(y_send(i, 4, view(0, (y + Y - 1) % Y), 1))
        item.append(y_send(i, 5, view(1, (y + 1) % Y), Y - 1))

    def finish(item):
        item[2][1].wait_recv()
        item[2][2].wait_recv()
        item[3].wait_recv()
        item[4].wait_recv()

    def thin_view(block):
        return lambda a, yy: outs[a].at[block, :, lane(yy)]

    def kv_view(base):
        return lambda a, yy: (k_out, v_out)[a].at[base + yy]

    settle(cot_y, cy, c_out)
    broad_step(0, 0)
    for copy in sums:
        copy.wait()
    total = sq[0]
    for k in range(1, 2 * X):
        total = total + sq[k]
    inverse = lax.rsqrt(total / D + EPS)
    inv_out[...] = inverse
    ey[y] = (x * inverse[:, :1] * gain[...].astype(F32)).astype(BF16)
    emb_y = [go(remote(ey.at[y], ey.at[y], y_s.at[1, k], y_r.at[1, k], wide=ypeer[k])) for k in range(1, Y)]
    settle(emb_y, ey, e_out)
    count = 2 * half - 1
    items, relayed = [], 0

    def spread_after(s):
        if s < half - 1:
            items.append(spread(2 * s, thin_view((z + zs - s - 1) % zs)))
            items.append(spread(2 * s + 1, thin_view((z + s + 1) % zs)))
        else:
            items.append(spread(2 * s, thin_view((z + half) % zs)))

    for s in range(half):
        ready = len(items)
        thin_step(s)
        if s > 0:
            spread_after(s - 1)
            broad_step(0, s)
        broad_step(1, s)
        for item in items[relayed:ready]:
            relay(item)
        relayed = ready
        if s == 0:
            for copy in pair:
                copy.wait_recv()
            items.append(spread(count, kv_view((z % 2) * Y)))
            items.append(spread(count + 1, kv_view(Y - (z % 2) * Y)))
    thin_step(half)
    spread_after(half - 1)
    for item in items[relayed:]:
        relay(item)
    for item in items:
        finish(item)
    for a in range(2):
        broad[a, a, half - 1].wait_recv()
    for copy in started:
        copy.wait_send()


def reduce_kernel(
    e_all, c_all, qw, kt, vt, ow, cosine, sine, out,
    away, home, pbuf, sbuf, rbuf,
    p_s, p_r, x_s, x_r, gx_s, gx_r, gp_s, gp_r,
):
    n = lax.axis_index("narrow")
    x, core = n // 2, n % 2
    twin = x * 2 + 1 - core
    xs = [(x + k) % X for k in range(X)]
    order = (2, 1, 3, 0)
    started = []

    def go(copy):
        copy.start()
        started.append(copy)
        return copy

    def project(side, into):
        blocks, width = e_all.shape[0] // 2, e_all.shape[2]
        part = pl.ds(side * blocks, blocks)
        e, c = (ref[part].reshape(-1, width) for ref in (e_all, c_all))
        keys, values = (ref[...].reshape(HDIM, width) for ref in (kt, vt))
        given = ((e, qw[...], 0), (e, keys, 1), (e, values, 1), (c, ow[...], 1))
        for i, (rows, weight, over) in enumerate(given):
            value = dot(rows, weight, 1, over)
            into[:, :, i * HDIM : (i + 1) * HDIM] = value.reshape(into.shape[:2] + (HDIM,))

    project(1 - core, away)
    first = {
        k: go(remote(away.at[xs[k]], pbuf.at[xs[k]], p_s.at[k], p_r.at[k], narrow=twin))
        for k in order
    }
    project(core, home)
    lo, hi = slice(0, 2 * HDIM), slice(2 * HDIM, 4 * HDIM)
    right, left = xs[1] * 2 + core, xs[X - 1] * 2 + core

    def pair_sum(k):
        first[k].wait_recv()
        return home[xs[k]] + pbuf[xs[k]]

    def hand(i, value, where):
        sbuf[i] = value
        return go(remote(sbuf.at[i], rbuf.at[i], x_s.at[i], x_r.at[i], narrow=where))

    value = pair_sum(2)
    chain_lo = hand(0, value[:, lo], right)
    chain_hi = hand(1, value[:, hi], left)
    value = pair_sum(1)
    near_hi = hand(2, value[:, hi], right)
    ahead = value[:, lo]
    value = pair_sum(3)
    near_lo = hand(3, value[:, lo], left)
    behind = value[:, hi]
    chain_lo.wait_recv()
    far_lo = hand(4, ahead + rbuf[0], right)
    chain_hi.wait_recv()
    far_hi = hand(5, behind + rbuf[1], left)
    value = pair_sum(0)
    near_lo.wait_recv()
    near_hi.wait_recv()
    total_lo = value[:, lo] + rbuf[3]
    total_hi = value[:, hi] + rbuf[2]
    far_lo.wait_recv()
    far_hi.wait_recv()
    total = jnp.concatenate([total_lo + rbuf[4], total_hi + rbuf[5]], 1)
    cos, sin = cosine[core, x], sine[core, x]
    for i in range(4):
        value = total[:, i * HDIM : (i + 1) * HDIM]
        if i < 2:
            value = value * cos + pltpu.roll(value, HDIM // 2, 1) * sin
        out[core, x, :, i * HDIM : (i + 1) * HDIM] = value.astype(BF16)
    mine = out.at[core, x]
    def give(i, here, where):
        return go(remote(here, here, gx_s.at[i], gx_r.at[i], narrow=where))

    given = [give(0, mine, right), give(1, mine, left)]
    shared = [go(remote(mine, mine, gp_s.at[0], gp_r.at[0], narrow=twin))]

    def share(k):
        block = out.at[core, xs[k]]
        shared.append(go(remote(block, block, gp_s.at[k], gp_r.at[k], narrow=twin)))

    given[0].wait_recv()
    far = [give(2, out.at[core, xs[3], :, lo], right)]
    share(3)
    given[1].wait_recv()
    far.append(give(3, out.at[core, xs[1], :, hi], left))
    share(1)
    for copy in far:
        copy.wait_recv()
    share(2)
    for copy in shared:
        copy.wait_recv()
    for copy in started:
        copy.wait_send()


def front_kernel(
    zs, emb, gain, cot, kw, vw, qw, ow, cosine, sine,
    out, k_out, v_out, inv_out,
    e_all, c_all, *scratch,
):
    gather_kernel(zs, emb, gain, cot, kw, vw, e_all, c_all, k_out, v_out, inv_out, *scratch[:17])
    reduce_kernel(e_all, c_all, qw, k_out, v_out, ow, cosine, sine, out, *scratch[17:])


def front(zs, emb, gain, cot, kw, vw, qw, ow, cosine, sine):
    rows, width = emb.shape
    block = Y * rows
    tokens, cols = zs * block, 4 * HDIM
    chunk = tokens // (2 * X)
    vmem = pl.BlockSpec(memory_space=pltpu.VMEM)
    dma = pltpu.SemaphoreType.DMA
    return pl.pallas_call(
        functools.partial(front_kernel, zs),
        out_shape=(
            jax.ShapeDtypeStruct((2, X, chunk, cols), BF16),
            jax.ShapeDtypeStruct((2 * Y,) + kw.shape, BF16),
            jax.ShapeDtypeStruct((2 * Y,) + vw.shape, BF16),
            jax.ShapeDtypeStruct((rows, 128), F32),
        ),
        in_specs=[vmem] * 9,
        out_specs=(vmem,) * 4,
        scratch_shapes=[
            pltpu.VMEM((zs, block, width), BF16),
            pltpu.VMEM((zs, block, width), BF16),
            pltpu.VMEM((rows, 128), F32),
            pltpu.VMEM((2 * X, rows, 128), F32),
            pltpu.VMEM((Y, rows, width), BF16),
            pltpu.VMEM((Y, rows, width), BF16),
            pltpu.VMEM((block, width), F32),
            dma((2 * X,)), dma((2 * X,)),
            dma((2, Y)), dma((2, Y)),
            dma((2, 2, zs // 2)), dma((2, 2, zs // 2)),
            dma((2, 2, zs // 2)), dma((2, 2, zs // 2)),
            dma((zs + 1, 6)), dma((zs + 1, 6)),
            dma((2,)), dma((2,)),
        ]
        + [pltpu.VMEM((X, chunk, cols), F32)] * 3
        + [pltpu.VMEM((6, chunk, cols // 2), F32)] * 2
        + [dma((X,))] * 2 + [dma((6,))] * 2 + [dma((X,))] * 4,
        compiler_params=pltpu.CompilerParams(collective_id=0, has_side_effects=True),
        name="front",
    )(
        emb, gain, cot, kw, vw, qw, ow,
        cosine.reshape(2, X, chunk, HDIM),
        sine.reshape(2, X, chunk, HDIM),
    )


def scatter_kernel(
    zs, gq, gk, gv, qw, kt, vt, emb, gain, inv, out,
    gn, sbuf, rbuf, stage, ysend, yrecv, in_own, inn,
    z_s, z_r, y_s, y_r, n_s, n_r,
):
    z, y, n, ypeer, up, down, npeer = places(zs)
    rows, width = emb.shape
    half = zs // 2
    meet([dict(narrow=npeer[k]) for k in range(1, 2 * X)]
         + [dict(wide=ypeer[k]) for k in range(1, Y)] + [dict(wide=up), dict(wide=down)])
    started = []

    def go(copy):
        copy.start()
        started.append(copy)
        return copy

    chain = {}
    groups = rbuf.shape[1]
    wid = width // groups
    lanes = [slice(h * wid, (h + 1) * wid) for h in range(groups)]
    for s in range(half):
        for h in range(groups):
            cut = lanes[h]
            if s == 0:
                value = dot(gq[...], qw[cut, :], 1, 1) + dot(gk[...], kt[:, cut], 1, 0)
                value = value + dot(gv[...], vt[:, cut], 1, 0)
                gn[:, :, cut] = value.reshape(zs, Y * rows, wid)
            for way in range(2):
                length = half if h % 2 == way else half - 1
                if s >= length:
                    continue
                far = length - s
                block = (z + far) % zs if way == 0 else (z + zs - far) % zs
                value = gn[block, :, cut]
                if s:
                    chain[way, h].wait_recv()
                    value = value + rbuf[way, h, s - 1].astype(F32)
                sbuf[way, h, s] = value.astype(BF16)
                chain[way, h] = go(
                    remote(
                        sbuf.at[way, h, s], rbuf.at[way, h, s], z_s.at[way, h, s], z_r.at[way, h, s],
                        wide=(up, down)[way],
                    )
                )
    last = []
    for h in range(groups):
        value = gn[z, :, lanes[h]]
        for way in range(2):
            length = half if h % 2 == way else half - 1
            chain[way, h].wait_recv()
            value = value + rbuf[way, h, length - 1].astype(F32)
        stage[:, lanes[h]] = value
        for j in range(Y):
            ysend[h, j] = stage[rows * j : rows * (j + 1), lanes[h]].astype(BF16)
        yrecv[h, y] = ysend[h, y]
        for k in (2, 1, 3):
            last.append(
                go(
                    remote(
                        ysend.at[h, (y + k) % Y], yrecv.at[h, y], y_s.at[h, k], y_r.at[h, k],
                        wide=ypeer[k],
                    )
                )
            )
    for copy in last:
        copy.wait_recv()
    sums = [
        (yrecv[h, 0].astype(F32) + yrecv[h, 1].astype(F32))
        + (yrecv[h, 2].astype(F32) + yrecv[h, 3].astype(F32))
        for h in range(groups)
    ]
    scaled = jnp.concatenate(sums, 1) * gain[...].astype(F32)
    inputs = emb[...].astype(F32)
    part = jnp.broadcast_to(jnp.sum(scaled * inputs, 1, keepdims=True), (rows, 128))
    sums = exchange_sums(part, n, npeer, in_own, inn, n_s, n_r)
    for copy in sums:
        copy.wait()
    inner = inn[0]
    for k in range(1, 2 * X):
        inner = inner + inn[k]
    inverse = inv[...]
    slope = (inverse * inverse * inverse * (inner / D))[:, :1]
    out[...] = (inverse[:, :1] * scaled - inputs * slope).astype(BF16)
    for copy in started:
        copy.wait_send()


def scatter(zs, gq, gk, gv, qw, kt, vt, emb, gain, inv):
    rows, width = emb.shape
    block = Y * rows
    vmem = pl.BlockSpec(memory_space=pltpu.VMEM)
    dma = pltpu.SemaphoreType.DMA
    half = zs // 2
    return pl.pallas_call(
        functools.partial(scatter_kernel, zs),
        out_shape=jax.ShapeDtypeStruct((rows, width), BF16),
        in_specs=[vmem] * 9,
        out_specs=vmem,
        scratch_shapes=[
            pltpu.VMEM((zs, block, width), F32),
            pltpu.VMEM((2, 4, half, block, width // 4), BF16),
            pltpu.VMEM((2, 4, half, block, width // 4), BF16),
            pltpu.VMEM((block, width), F32),
            pltpu.VMEM((4, Y, rows, width // 4), BF16),
            pltpu.VMEM((4, Y, rows, width // 4), BF16),
            pltpu.VMEM((rows, 128), F32),
            pltpu.VMEM((2 * X, rows, 128), F32),
            dma((2, 4, half)), dma((2, 4, half)),
            dma((4, Y)), dma((4, Y)),
            dma((2 * X,)), dma((2 * X,)),
        ],
        compiler_params=pltpu.CompilerParams(collective_id=2, has_side_effects=True),
        name="scatter",
    )(gq, gk, gv, qw, kt, vt, emb, gain, inv)


def rotary_tables(segment_ids):
    spots = jnp.arange(segment_ids.shape[0], dtype=jnp.int32)
    starts = jnp.sum((segment_ids[None, :] < segment_ids[:, None]).astype(jnp.int32), 1)
    position = (spots - starts).astype(F32)
    half = HDIM // 2
    frequency = jnp.exp(-(2.0 * jnp.arange(half, dtype=F32) / HDIM) * math.log(THETA))
    angle = position[:, None] * frequency[None, :]
    cosine, sine = jnp.cos(angle), jnp.sin(angle)
    return jnp.concatenate([cosine, cosine], 1), jnp.concatenate([-sine, sine], 1)


def swap(values):
    half = HDIM // 2
    return jnp.concatenate([values[:, half:], values[:, :half]], 1)


def dot(a, b, da, db):
    return lax.dot_general(a, b, (((da,), (db,)), ((), ())), preferred_element_type=F32)


def head_grads(q, k, v, g, allowed, scale):
    scores = jnp.where(allowed, dot(q, k, 1, 1) * scale, -1e30)
    raised = jnp.exp(scores - jnp.max(scores, 1, keepdims=True))
    attend = raised / jnp.sum(raised, 1, keepdims=True)
    grad_attend = dot(g, v, 1, 1)
    centre = jnp.sum(attend * grad_attend, 1, keepdims=True)
    grad_scores = (attend * (grad_attend - centre) * scale).astype(BF16)
    return (
        dot(grad_scores, k, 1, 0),
        dot(grad_scores, q, 0, 0),
        dot(attend.astype(BF16), g, 0, 0),
    )


def local(emb, norm_gain, query_weight, key_weight, value_weight, output_weight, segment_ids, cot):
    zs = lax.axis_size("wide") // Y
    total = segment_ids.shape[0]
    gain = norm_gain[None, :]
    width = emb.shape[1]
    cosine, sine = rotary_tables(segment_ids)
    heads, kt, vt, inv = front(
        zs, emb, gain, cot, key_weight.T, value_weight.T, query_weight, output_weight, cosine, sine
    )
    heads = heads.reshape(total, 4 * HDIM)
    kt, vt = kt.reshape(HDIM, width), vt.reshape(HDIM, width)
    q, k, v, g = (heads[:, i * HDIM : (i + 1) * HDIM] for i in range(4))
    spots = jnp.arange(total, dtype=jnp.int32)
    allowed = (segment_ids[:, None] == segment_ids[None, :]) & (spots[None, :] <= spots[:, None])
    gq, gk, gv = head_grads(q, k, v, g, allowed, HDIM ** (-0.5))
    gq = (gq * cosine - swap(gq) * sine).astype(BF16)
    gk = (gk * cosine - swap(gk) * sine).astype(BF16)
    return scatter(zs, gq, gk, gv.astype(BF16), query_weight, kt, vt, emb, gain, inv)


def solution(mesh):
    return jax.shard_map(
        local,
        mesh=mesh,
        in_specs=(
            P("wide", "narrow"),
            P("narrow"),
            P("narrow", "wide"),
            P("narrow", "wide"),
            P("narrow", "wide"),
            P("wide", "narrow"),
            P(),
            P("wide", "narrow"),
        ),
        out_specs=P("wide", "narrow"),
        check_vma=False,
    )
```
